32 devices in a mesh: band: 2 (over y), slab: 16 (over z, x, core).
Axes of the slice: x: 2, y: 2, z: 4, core: 2. Of those that a mesh axis runs over, the one named last changes fastest.
Arguments:
- own_orbitals: float32 [4, 128, 128, 128], P('band', 'slab'), may hold values from -6 to 6
- partners: float32 [8, 128, 128, 128], P('band', 'slab'), may hold values from -6 to 6
Outputs:
- own_field: float32 [4, 128, 128, 128], P('band', 'slab')
- partner_field: float32 [8, 128, 128, 128], P('band', 'slab')
The draws below stay inside these ranges and needn't reach their ends.
All inputs are finite; a program needn't handle non-finite values.
Results may differ from the reference program's by a relative error of at most 0.0001.
Values sent between devices are 32-bit elements; how exact they have to be, the bound alone decides.
No kernel may reach another device: no remote copies, remote signals or barrier semaphores. Data moves between devices by JAX's collectives and lax.ppermute only.
A program may use at most 128 MiB of HBM per device.

```python
import math
import jax
import jax.numpy as jnp

NG = 128
OWN_DEV = 2
PART_DEV = 4
STEPS = 2
BANDS = 4
PARTNERS = 8


def level_of(own_key, extent, shards, least, high):
    gain = 1.0
    for position, blocks in shards:
        heights = jax.random.uniform(jax.random.fold_in(jax.random.fold_in(own_key, 6), position), (blocks,), jnp.float32, least / len(shards), high / len(shards))
        gain = gain * jnp.repeat(jnp.exp(heights), extent[position] // blocks).reshape((-1,) + (1,) * (len(extent) - 1 - position))
    return gain


def noise(key, shape, deviation, bound, split=(), held_as=jnp.bfloat16):
    values = jax.random.normal(key, shape, jnp.float32) * deviation
    if len(split) > 0:
        values = level_of(key, shape, split, -0.22, 0.18) * values
    return jnp.clip(values, min=-bound, max=bound).astype(held_as)


def setup_inputs(seed: int = 0) -> dict:
    splits = jax.random.split(jax.random.key(seed), 3)
    own_orbitals = noise(splits[0], (BANDS, NG, NG, NG), 1.0, 6.0, ((0, 2), (1, 16)), jnp.float32)
    partners = noise(splits[1], (PARTNERS, NG, NG, NG), 1.0, 6.0, ((0, 2), (1, 16)), jnp.float32)
    return dict(own_orbitals=own_orbitals, partners=partners)


coulomb_scale = 46.9 * 46.9 / math.pi


def kernel_table():
    waves = jnp.fft.fftfreq(NG) * NG
    square = waves[:, None, None] * waves[:, None, None] + waves[None, :, None] * waves[None, :, None] + waves[None, None, :] * waves[None, None, :]
    return jnp.where(square > 0, coulomb_scale / jnp.maximum(square, 1.0), 0.0)


def reference(own_orbitals, partners):
    groups = own_orbitals.shape[0] // OWN_DEV
    kernel = kernel_table()
    own_sets = own_orbitals.reshape((groups, OWN_DEV, NG, NG, NG))
    part_sets = partners.reshape((groups, PART_DEV, NG, NG, NG))
    own_out = [jnp.zeros((OWN_DEV, NG, NG, NG), jnp.float32) for group_id in range(groups)]
    part_out = [jnp.zeros((PART_DEV, NG, NG, NG), jnp.float32) for group_id in range(groups)]
    for group_id in range(groups):
        for step_no in range(1, STEPS + 1):
            block_id = (group_id - step_no) % groups
            orbitals = own_sets[group_id]
            partner_set = part_sets[block_id]
            density = orbitals[:, None] * partner_set[None]
            spectrum = jnp.fft.fftn(density, axes=(2, 3, 4)) * kernel
            potential = jnp.real(jnp.fft.ifftn(spectrum, axes=(2, 3, 4))).astype(jnp.float32)
            own_out[group_id] = own_out[group_id] + jnp.sum(potential * partner_set[None], axis=1)
            part_out[block_id] = part_out[block_id] + jnp.sum(potential * orbitals[:, None], axis=0)
    return jnp.concatenate(own_out, 0), jnp.concatenate(part_out, 0)
```

```python
import functools
import math

import jax
import jax.numpy as jnp
import numpy as np
from jax import lax
from jax.sharding import PartitionSpec as P

STEPS = 2


coulomb_scale = 46.9 * 46.9 / math.pi
precision = lax.Precision.HIGH


def cas_table(length):
    half = length // 2
    angles = np.arange(half) * (2.0 * math.pi / length)
    first = (np.cos(angles) + np.sin(angles)).astype(np.float32)
    wave = np.concatenate([first, -first])
    positions = np.arange(length)
    return wave[(positions[:, None] * positions[None, :]) % length]


def apply_table(pattern, field, table):
    return jnp.einsum(pattern, field, table, precision=precision)


def frequency(positions, length):
    return jnp.where(positions < length // 2, positions, positions - length).astype(jnp.float32)


def coulomb(z_waves, y_waves, x_waves, cells):
    square = (
        z_waves[:, None, None] * z_waves[:, None, None]
        + y_waves[None, :, None] * y_waves[None, :, None]
        + x_waves[None, None, :] * x_waves[None, None, :]
    )
    return jnp.where(square > 0, (coulomb_scale / float(cells)) / jnp.maximum(square, 1.0), 0.0)


def band_shift(block, groups, distance):
    if distance % groups == 0:
        return block
    route = [((b + distance) % groups, b) for b in range(groups)]
    return lax.ppermute(block, "band", route)


def pencils(own, partners, groups, slabs):
    length = own.shape[3]
    own_count, part_count = own.shape[0], partners.shape[0]
    table = jnp.asarray(cas_table(length))
    rows_y = length // slabs
    waves = frequency(lax.iota(jnp.int32, length), length)
    y_waves = frequency(
        lax.axis_index("slab") * rows_y + lax.iota(jnp.int32, rows_y), length
    )
    kernel = coulomb(waves, y_waves, waves, length**3)
    own_acc = jnp.zeros(own.shape, jnp.float32)
    part_acc = jnp.zeros(partners.shape, jnp.float32)
    for step_no in sorted(range(1, STEPS + 1), key=lambda s: s % groups != 0):
        bands = band_shift(own, groups, step_no)
        field = (bands[:, None] * partners[None]).reshape((-1,) + own.shape[1:])
        field = apply_table("pzyx,xk->pzyk", field, table)
        field = apply_table("pzyx,yk->pzkx", field, table)
        field = lax.all_to_all(field, "slab", split_axis=2, concat_axis=1, tiled=True)
        field = apply_table("pzyx,zk->pkyx", field, table) * kernel
        field = apply_table("pzyx,zk->pkyx", field, table)
        field = lax.all_to_all(field, "slab", split_axis=1, concat_axis=2, tiled=True)
        field = apply_table("pzyx,yk->pzkx", field, table)
        field = apply_table("pzyx,xk->pzyk", field, table)
        potential = field.reshape((own_count, part_count) + own.shape[1:])
        part_acc = part_acc + jnp.sum(potential * bands[:, None], axis=0)
        own_add = jnp.sum(potential * partners[None], axis=1)
        own_acc = own_acc + band_shift(own_add, groups, -step_no)
    return own_acc, part_acc


def solution(mesh):
    groups, slabs = mesh.shape["band"], mesh.shape["slab"]
    spec = P("band", "slab", None, None)
    return jax.shard_map(
        functools.partial(pencils, groups=groups, slabs=slabs),
        mesh=mesh, in_specs=(spec, spec), out_specs=(spec, spec), check_vma=False,
    )
```

```python
import math

import jax
import jax.numpy as jnp
import numpy as np
from jax import lax
from jax.sharding import PartitionSpec as P

STEPS = 2
CHUNKS = 4


coulomb_scale = 46.9 * 46.9 / math.pi
precision = lax.Precision.HIGH


def cas_table(length):
    half = length // 2
    angles = np.arange(half) * (2.0 * math.pi / length)
    first = (np.cos(angles) + np.sin(angles)).astype(np.float32)
    wave = np.concatenate([first, -first])
    positions = np.arange(length)
    return wave[(positions[:, None] * positions[None, :]) % length]


def apply_table(pattern, field, table):
    return jnp.einsum(pattern, field, table, precision=precision)


def frequency(positions, length):
    return jnp.where(positions < length // 2, positions, positions - length).astype(jnp.float32)


def coulomb(z_waves, y_waves, x_waves, cells):
    square = (
        z_waves[:, None, None] * z_waves[:, None, None]
        + y_waves[None, :, None] * y_waves[None, :, None]
        + x_waves[None, None, :] * x_waves[None, None, :]
    )
    return jnp.where(square > 0, (coulomb_scale / float(cells)) / jnp.maximum(square, 1.0), 0.0)


def band_shift(block, groups, distance):
    if distance % groups == 0:
        return block
    route = [((b + distance) % groups, b) for b in range(groups)]
    return lax.ppermute(block, "band", route)


def pencils(own, partners, groups, slabs):
    length = own.shape[3]
    own_count, part_count = own.shape[0], partners.shape[0]
    table = jnp.asarray(cas_table(length))
    rows_y = length // slabs
    waves = frequency(lax.iota(jnp.int32, length), length)
    y_waves = frequency(
        lax.axis_index("slab") * rows_y + lax.iota(jnp.int32, rows_y), length
    )
    kernel = coulomb(waves, y_waves, waves, length**3)
    own_acc = jnp.zeros(own.shape, jnp.float32)
    part_acc = jnp.zeros(partners.shape, jnp.float32)
    for step_no in sorted(range(1, STEPS + 1), key=lambda s: s % groups != 0):
        bands = band_shift(own, groups, step_no)
        field = (bands[:, None] * partners[None]).reshape((-1,) + own.shape[1:])
        field = apply_table("pzyx,xk->pzyk", field, table)
        field = apply_table("pzyx,yk->pzkx", field, table)
        field = lax.all_to_all(field, "slab", split_axis=2, concat_axis=1, tiled=True)
        field = apply_table("pzyx,zk->pkyx", field, table) * kernel
        field = apply_table("pzyx,zk->pkyx", field, table)
        field = lax.all_to_all(field, "slab", split_axis=1, concat_axis=2, tiled=True)
        field = apply_table("pzyx,yk->pzkx", field, table)
        field = apply_table("pzyx,xk->pzyk", field, table)
        potential = field.reshape((own_count, part_count) + own.shape[1:])
        part_acc = part_acc + jnp.sum(potential * bands[:, None], axis=0)
        own_add = jnp.sum(potential * partners[None], axis=1)
        own_acc = own_acc + band_shift(own_add, groups, -step_no)
    return own_acc, part_acc


def whole_fields(own, partners, groups, slabs, chunks):
    length = own.shape[3]
    rows = own.shape[1]
    table = jnp.asarray(cas_table(length))
    me = lax.axis_index("slab")
    part_half, own_band, part_low = (me >> 3) & 1, (me >> 2) & 1, (me >> 1) & 1

    def swap(block, mask):
        return lax.ppermute(block, "slab", [(i ^ mask, i) for i in range(slabs)])

    def across(block, flip, back):
        route = []
        for b in range(groups):
            for i in range(slabs):
                source = ((b + 1 + (i & 1)) % groups) * slabs + (i ^ flip)
                target = b * slabs + i
                route.append((target, source) if back else (source, target))
        return lax.ppermute(block, ("band", "slab"), route)

    def pick(block, position, axis=0):
        return lax.dynamic_index_in_dim(block, position, axis, keepdims=False)

    def ordered(position, mine, other):
        return jnp.where(position == 0, jnp.stack([mine, other]), jnp.stack([other, mine]))

    def own_in(block):
        block = jnp.stack([pick(block, own_band), swap(pick(block, 1 - own_band), 4)])
        block = jnp.stack([block, swap(block, 8)])
        block = jnp.stack([block, swap(block, 2)])
        return across(block, 0, False), across(block, 1, False)

    def part_in(block):
        block = block.reshape((2, 2) + block.shape[1:])
        block = jnp.stack([pick(block, part_half), swap(pick(block, 1 - part_half), 8)], 1)
        block = jnp.stack([pick(block, part_low), swap(pick(block, 1 - part_low), 2)])
        block = jnp.stack([block, swap(block, 4)], 2)
        return block, swap(block, 1)

    def own_back(first, second):
        block = across(first, 0, True) + across(second, 1, True)
        block = block[0] + swap(block[1], 2)
        block = block[0] + swap(block[1], 8)
        return ordered(own_band, block[0], swap(block[1], 4))

    def part_back(first, second):
        block = first + swap(second, 1)
        block = block[:, :, 0] + swap(block[:, :, 1], 4)
        block = ordered(part_low, block[0], swap(block[1], 2))
        block = ordered(part_half, block[:, 0], swap(block[:, 1], 8))
        return block.reshape((-1,) + block.shape[2:])

    cut = length // chunks
    pieces = [slice(k * cut, (k + 1) * cut) for k in range(chunks)]
    own_pairs = [own_in(own[:, :, piece]) for piece in pieces]
    part_pairs = [part_in(partners[:, :, piece]) for piece in pieces]

    def laid(pair):
        return [half.reshape((-1,) + half.shape[-2:]) for half in pair]

    own_pairs = [laid(pair) for pair in own_pairs]
    part_pairs = [laid(pair) for pair in part_pairs]
    field = jnp.concatenate(
        [
            apply_table("zyx,xk->zyk", jnp.concatenate([a * b for a, b in zip(o, p)]), table)
            for o, p in zip(own_pairs, part_pairs)
        ],
        1,
    )
    position = lax.iota(jnp.int32, slabs)
    slab_of = me ^ (
        (position & 1) * 4 + (position & 2) * 4 + (position & 4) // 2 + (position & 8) // 8
    )
    z_table = jnp.take(table.reshape(slabs, rows, length), slab_of, axis=0).reshape(length, length)
    waves = frequency(lax.iota(jnp.int32, length), length)
    kernel = coulomb(waves, waves, waves, length**3)
    field = apply_table("zyx,yk->zkx", field, table)
    field = apply_table("zyx,zk->kyx", field, z_table) * kernel
    field = apply_table("kyx,zk->zyx", field, z_table)
    field = apply_table("zyx,yk->zkx", field, table)
    own_out, part_out = [], []
    parts_shape = (2, 2, 2, rows, cut, length)
    for k, piece in enumerate(pieces):
        potential = apply_table("zyx,xk->zyk", field[:, piece], table)
        halves = [potential[: length // 2], potential[length // 2 :]]
        own_out.append(own_back(*[(v * b).reshape(parts_shape) for v, b in zip(halves, part_pairs[k])]))
        part_out.append(part_back(*[(v * a).reshape(parts_shape) for v, a in zip(halves, own_pairs[k])]))
    return jnp.concatenate(own_out, 2), jnp.concatenate(part_out, 2)


def solution(mesh):
    groups, slabs = mesh.shape["band"], mesh.shape["slab"]
    spec = P("band", "slab", None, None)

    def shards(own, partners):
        if slabs == 16 and own.shape[0] == 2 and partners.shape[0] == 4 and STEPS == 2:
            return whole_fields(own, partners, groups, slabs, CHUNKS)
        return pencils(own, partners, groups, slabs)

    return jax.shard_map(
        shards, mesh=mesh, in_specs=(spec, spec), out_specs=(spec, spec), check_vma=False
    )
```

```python
import math

import jax
import jax.numpy as jnp
import ml_dtypes
import numpy as np
from jax import lax
from jax.experimental import pallas as pl
from jax.experimental.pallas import tpu as pltpu
from jax.sharding import PartitionSpec as P

STEPS = 2


coulomb_scale = 46.9 * 46.9 / math.pi
precision = lax.Precision.HIGH


def cas_table(length):
    half = length // 2
    angles = np.arange(half) * (2.0 * math.pi / length)
    first = (np.cos(angles) + np.sin(angles)).astype(np.float32)
    wave = np.concatenate([first, -first])
    positions = np.arange(length)
    return wave[(positions[:, None] * positions[None, :]) % length]


def apply_table(pattern, field, table):
    return jnp.einsum(pattern, field, table, precision=precision)


def frequency(positions, length):
    return jnp.where(positions < length // 2, positions, positions - length).astype(jnp.float32)


def coulomb(z_waves, y_waves, x_waves, cells):
    square = (
        z_waves[:, None, None] * z_waves[:, None, None]
        + y_waves[None, :, None] * y_waves[None, :, None]
        + x_waves[None, None, :] * x_waves[None, None, :]
    )
    return jnp.where(square > 0, (coulomb_scale / float(cells)) / jnp.maximum(square, 1.0), 0.0)


def band_shift(block, groups, distance):
    if distance % groups == 0:
        return block
    route = [((b + distance) % groups, b) for b in range(groups)]
    return lax.ppermute(block, "band", route)


def pencils(own, partners, groups, slabs):
    length = own.shape[3]
    own_count, part_count = own.shape[0], partners.shape[0]
    table = jnp.asarray(cas_table(length))
    rows_y = length // slabs
    waves = frequency(lax.iota(jnp.int32, length), length)
    y_waves = frequency(
        lax.axis_index("slab") * rows_y + lax.iota(jnp.int32, rows_y), length
    )
    kernel = coulomb(waves, y_waves, waves, length**3)
    own_acc = jnp.zeros(own.shape, jnp.float32)
    part_acc = jnp.zeros(partners.shape, jnp.float32)
    for step_no in sorted(range(1, STEPS + 1), key=lambda s: s % groups != 0):
        bands = band_shift(own, groups, step_no)
        field = (bands[:, None] * partners[None]).reshape((-1,) + own.shape[1:])
        field = apply_table("pzyx,xk->pzyk", field, table)
        field = apply_table("pzyx,yk->pzkx", field, table)
        field = lax.all_to_all(field, "slab", split_axis=2, concat_axis=1, tiled=True)
        field = apply_table("pzyx,zk->pkyx", field, table) * kernel
        field = apply_table("pzyx,zk->pkyx", field, table)
        field = lax.all_to_all(field, "slab", split_axis=1, concat_axis=2, tiled=True)
        field = apply_table("pzyx,yk->pzkx", field, table)
        field = apply_table("pzyx,xk->pzyk", field, table)
        potential = field.reshape((own_count, part_count) + own.shape[1:])
        part_acc = part_acc + jnp.sum(potential * bands[:, None], axis=0)
        own_add = jnp.sum(potential * partners[None], axis=1)
        own_acc = own_acc + band_shift(own_add, groups, -step_no)
    return own_acc, part_acc


def two_terms(values):
    high = values.astype(jnp.bfloat16)
    return high, (values - high.astype(jnp.float32)).astype(jnp.bfloat16)


def table_terms(length):
    table = cas_table(length)
    high = table.astype(ml_dtypes.bfloat16)
    low = (table - high.astype(np.float32)).astype(ml_dtypes.bfloat16)
    return high, low


def from_left(high, low, xp=np):
    return xp.concatenate([xp.concatenate([high, high], 1), xp.concatenate([low, low], 1)], 0)


def product(left, right):
    return jnp.dot(left, right, preferred_element_type=jnp.float32)


def along_x(rows, right):
    high, low = two_terms(rows)
    both = product(jnp.concatenate([high, low], 1), right)
    return both[:, : both.shape[1] // 2] + both[:, both.shape[1] // 2 :]


def along_y(columns, left):
    high, low = two_terms(columns)
    both = product(left, jnp.concatenate([high, low], 0))
    return both[: both.shape[0] // 2] + both[both.shape[0] // 2 :]


def slab_pieces(step, refs):
    first, fx_a, fx_b, second, sx_a, sx_b, parts, parts_c = refs
    return [
        (0, (first,), parts),
        (1, (fx_a, fx_b), parts),
        (2, (second,), parts_c),
        (3, (sx_a, sx_b), parts_c),
    ]


def gather_kernel(right_ref, left_ref, *refs):
    pieces, out_ref, pair_ref = refs[:8], refs[8], refs[9]
    step = pl.program_id(0)
    rows, length = pair_ref.shape[0], pair_ref.shape[1]
    for turn, own_refs, part_ref in slab_pieces(step, pieces):

        @pl.when(step // 2 == turn)
        def _(own_refs=own_refs, part_ref=part_ref):
            count = rows // len(own_refs)
            for k, own_ref in enumerate(own_refs):
                span = pl.ds(k * count, count)
                pair_ref[span] = own_ref[0] * part_ref[0, span]

    flat_out = out_ref.reshape(rows * length, length)
    for r in range(0, rows, 2):
        block = along_x(pair_ref[pl.ds(r, 2)].reshape(2 * length, length), right_ref[...])
        block = along_y(jnp.concatenate([block[:length], block[length:]], 1), left_ref[...])
        flat_out[pl.ds(r, length, stride=rows), :] = block[:, :length]
        flat_out[pl.ds(r + 1, length, stride=rows), :] = block[:, length:]


def column_kernel(left_ref, back_ref, coulomb_ref, a_ref, b_ref, a_out, b_out):
    count, half, length = a_ref.shape
    for k in range(0, count, 2):
        block = jnp.concatenate(
            [
                jnp.concatenate([a_ref[k], b_ref[k]], 0),
                jnp.concatenate([a_ref[k + 1], b_ref[k + 1]], 0),
            ],
            1,
        )
        block = along_y(block, left_ref[...])
        block = block * jnp.concatenate([coulomb_ref[k], coulomb_ref[k + 1]], 1)
        block = along_y(block, back_ref[...])
        for j in range(2):
            piece = block[:, j * length : (j + 1) * length]
            a_out[k + j] = piece[:half]
            b_out[k + j] = piece[half:]


def scatter_kernel(right_ref, left_ref, field_ref, *refs):
    pieces, outs, pot_ref = refs[:8], refs[-9:-1], refs[-1]
    step = pl.program_id(0)
    rows, length = pot_ref.shape[0], pot_ref.shape[1]
    flat = field_ref.reshape(rows * length, length)
    for r in range(0, rows, 2):
        block = jnp.concatenate(
            [flat[pl.ds(r, length, stride=rows), :], flat[pl.ds(r + 1, length, stride=rows), :]], 1
        )
        block = along_y(block, left_ref[...])
        block = jnp.concatenate([block[:, :length], block[:, length:]], 0)
        pot_ref[pl.ds(r, 2)] = along_x(block, right_ref[...]).reshape(2, length, length)
    for (turn, own_refs, part_ref), (_, own_outs, part_out) in zip(
        slab_pieces(step, pieces), slab_pieces(step, outs)
    ):

        @pl.when(step // 2 == turn)
        def _(own_refs=own_refs, part_ref=part_ref, own_outs=own_outs, part_out=part_out):
            count = rows // len(own_refs)
            for k, (own_ref, own_out) in enumerate(zip(own_refs, own_outs)):
                span = pl.ds(k * count, count)
                own_out[0] = pot_ref[span] * part_ref[0, span]
                part_out[0, span] = pot_ref[span] * own_ref[0]


def piece_specs(rows, length, z_low):
    def own_spec(turn, count):
        return pl.BlockSpec(
            (1, count, length, length),
            lambda i: (jnp.clip(i - 2 * turn, 0, 1) * 2 + z_low, 0, 0, 0),
        )

    def part_spec(core):
        return pl.BlockSpec(
            (1, rows, length, length), lambda i: (jnp.clip(i - 4 * core, 0, 3), 0, 0, 0)
        )

    half = rows // 2
    return [
        own_spec(0, rows), own_spec(1, half), own_spec(1, half),
        own_spec(2, rows), own_spec(3, half), own_spec(3, half),
        part_spec(0), part_spec(1),
    ]


def fixed_spec(shape):
    return pl.BlockSpec(shape, lambda i: (0,) * len(shape))


def settings(megabytes):
    return pltpu.CompilerParams(
        dimension_semantics=("arbitrary",), vmem_limit_bytes=megabytes * 2**20
    )


def cost(length, fields, transforms):
    cells = length**3
    return pl.CostEstimate(
        flops=transforms * 8 * cells * length, bytes_accessed=4 * fields * cells, transcendentals=0
    )


def gather_half(right, left, pieces, z_low):
    rows, length = pieces[0].shape[1], pieces[0].shape[2]
    return pl.pallas_call(
        gather_kernel,
        grid=(8,),
        in_specs=[fixed_spec(right.shape), fixed_spec(left.shape)] + piece_specs(rows, length, z_low),
        out_specs=pl.BlockSpec((length, rows, length), lambda i: (0, i, 0)),
        out_shape=jax.ShapeDtypeStruct((length, 8 * rows, length), jnp.float32),
        scratch_shapes=[pltpu.VMEM((rows, length, length), jnp.float32)],
        compiler_params=settings(32),
        cost_estimate=cost(length, 2, 1),
    )(right, left, *pieces)


def columns(left, back, coulomb_table, a, b):
    length, half = a.shape[0], a.shape[1]
    count = 8
    block = pl.BlockSpec((count, half, length), lambda i: (i, 0, 0))
    return pl.pallas_call(
        column_kernel,
        grid=(length // count,),
        in_specs=[
            fixed_spec(left.shape), fixed_spec(back.shape),
            pl.BlockSpec((count, length, length), lambda i: (i, 0, 0)), block, block,
        ],
        out_specs=[block, block],
        out_shape=[jax.ShapeDtypeStruct(a.shape, jnp.float32)] * 2,
        compiler_params=settings(32),
        cost_estimate=cost(length, 3, 2),
    )(left, back, coulomb_table, a, b)


def scatter_half(right, left, field, pieces, z_low, held):
    rows, length = pieces[0].shape[1], pieces[0].shape[2]
    specs = piece_specs(rows, length, z_low)
    count = len(held)
    return pl.pallas_call(
        scatter_kernel,
        grid=(8,),
        in_specs=[
            fixed_spec(right.shape), fixed_spec(left.shape),
            pl.BlockSpec((length, rows, length), lambda i: (0, i, 0)),
        ]
        + specs
        + [pl.BlockSpec(memory_space=pl.ANY)] * count,
        out_specs=specs,
        out_shape=[jax.ShapeDtypeStruct(piece.shape, jnp.float32) for piece in pieces],
        input_output_aliases={11 + k: k for k in range(count)},
        scratch_shapes=[pltpu.VMEM((rows, length, length), jnp.float32)],
        compiler_params=settings(48),
        cost_estimate=cost(length, 3, 1),
    )(right, left, field, *pieces, *held)


def whole_fields(own, partners, groups, slabs):
    length = own.shape[3]
    rows = own.shape[1]
    half = rows // 2
    plane = own.shape[2:]
    me = lax.axis_index("slab")
    part_half, own_band, part_low = (me >> 3) & 1, (me >> 2) & 1, (me >> 1) & 1

    def swap(block, mask):
        return lax.ppermute(block, "slab", [(i ^ mask, i) for i in range(slabs)])

    def across(block, flip, back):
        route = []
        for b in range(groups):
            for i in range(slabs):
                source = ((b + 1 + (i & 1)) % groups) * slabs + (i ^ flip)
                target = b * slabs + i
                route.append((target, source) if back else (source, target))
        return lax.ppermute(block, ("band", "slab"), route)

    def pick(block, position, axis=0):
        return lax.dynamic_index_in_dim(block, position, axis, keepdims=False)

    def ordered(position, mine, other, axis=0):
        return jnp.where(
            position == 0, jnp.stack([mine, other], axis), jnp.stack([other, mine], axis)
        )

    def together(*blocks):
        return lax.optimization_barrier(blocks)

    high, low = table_terms(length)
    left = jnp.asarray(from_left(high, low))
    right = jnp.asarray(from_left(high, low).T)
    position = lax.iota(jnp.int32, slabs)
    slab_of = me ^ (
        (position & 1) * 8 + (position & 2) + (position & 4) // 4 + (position & 8) // 2
    )
    z_high, z_low = [
        jnp.take(jnp.asarray(term).reshape(slabs, rows, length), slab_of, axis=0).reshape(
            length, length
        )
        for term in (high, low)
    ]
    z_left, z_back = from_left(z_high.T, z_low.T, jnp), from_left(z_high, z_low, jnp)
    waves = frequency(lax.iota(jnp.int32, length), length)
    coulomb_table = coulomb(waves, waves, waves, length**3)

    kept, passed = pick(own, own_band), pick(own, 1 - own_band)
    bands = jnp.stack([kept, swap(passed, 4), swap(kept, 8), swap(passed, 12)])
    parts = partners.reshape((2, 2) + partners.shape[1:])
    parts = jnp.stack([pick(parts, part_low, 1), swap(pick(parts, 1 - part_low, 1), 2)])
    bands, parts = together(bands, parts)
    bands_x = swap(bands, 2)
    first, second = across(bands, 0, False), across(bands, 1, False)
    parts = jnp.stack([pick(parts, part_half, 1), swap(pick(parts, 1 - part_half, 1), 8)], 1)
    bands_x, first, second, parts = together(bands_x, first, second, parts)
    parts = parts.reshape((4, rows) + plane)
    parts_z, parts_c = swap(parts, 4), swap(parts, 1)
    fx_a, fx_b = across(bands_x[:, :half], 0, False), swap(first[:, half:], 2)
    sx_a, sx_b = across(bands_x[:, :half], 1, False), swap(second[:, half:], 2)
    own_pieces = [first, fx_a, fx_b, second, sx_a, sx_b]
    even = own_pieces + [parts, parts_c]
    field_even = gather_half(right, left, even, 0)
    odd = own_pieces + [parts_z, swap(parts_z, 1)]
    field_odd = gather_half(right, left, odd, 1)

    field_even, field_odd = columns(z_left, z_back, coulomb_table, field_even, field_odd)

    *own_pieces, parts_z, parts_zc = scatter_half(right, left, field_odd, odd, 1, [])
    parts_z = parts_z + swap(parts_zc, 1)
    parts_z = swap(parts_z, 4)
    *own_pieces, parts, parts_c = scatter_half(right, left, field_even, even, 0, own_pieces)
    first, fx_a, fx_b, second, sx_a, sx_b = own_pieces
    bands_x = across(fx_a, 0, True) + across(sx_a, 1, True)
    fx_b, sx_b = swap(fx_b, 2), swap(sx_b, 2)
    parts = (parts + swap(parts_c, 1) + parts_z).reshape((2, 2, rows) + plane)
    first = jnp.concatenate([first[:, :half], first[:, half:] + fx_b], 1)
    second = jnp.concatenate([second[:, :half], second[:, half:] + sx_b], 1)
    bands_x, first, second, parts = together(bands_x, first, second, parts)
    bands = across(first, 0, True) + across(second, 1, True)
    bands_x = swap(bands_x, 2)
    bands = jnp.concatenate([bands[:, :half] + bands_x, bands[:, half:]], 1)
    parts = ordered(part_half, parts[:, 0], swap(parts[:, 1], 8), 1)
    bands, parts = together(bands, parts)
    kept = bands[0] + swap(bands[2], 8)
    passed = swap(bands[1], 4) + swap(bands[3], 12)
    parts = ordered(part_low, parts[0], swap(parts[1], 2), 1)
    return ordered(own_band, kept, passed), parts.reshape(partners.shape)


def solution(mesh):
    groups, slabs = mesh.shape["band"], mesh.shape["slab"]
    spec = P("band", "slab", None, None)

    def shards(own, partners):
        if slabs == 16 and own.shape[0] == 2 and partners.shape[0] == 4 and STEPS == 2:
            return whole_fields(own, partners, groups, slabs)
        return pencils(own, partners, groups, slabs)

    return jax.shard_map(
        shards, mesh=mesh, in_specs=(spec, spec), out_specs=(spec, spec), check_vma=False
    )
```

```python
import math

import jax
import jax.numpy as jnp
import ml_dtypes
import numpy as np
from jax import lax
from jax.experimental import pallas as pl
from jax.experimental.pallas import tpu as pltpu
from jax.sharding import PartitionSpec as P

STEPS = 2


coulomb_scale = 46.9 * 46.9 / math.pi
precision = lax.Precision.HIGH


def cas_table(length):
    half = length // 2
    angles = np.arange(half) * (2.0 * math.pi / length)
    first = (np.cos(angles) + np.sin(angles)).astype(np.float32)
    wave = np.concatenate([first, -first])
    positions = np.arange(length)
    return wave[(positions[:, None] * positions[None, :]) % length]


def apply_table(pattern, field, table):
    return jnp.einsum(pattern, field, table, precision=precision)


def frequency(positions, length):
    return jnp.where(positions < length // 2, positions, positions - length).astype(jnp.float32)


def coulomb(z_waves, y_waves, x_waves, cells):
    square = (
        z_waves[:, None, None] * z_waves[:, None, None]
        + y_waves[None, :, None] * y_waves[None, :, None]
        + x_waves[None, None, :] * x_waves[None, None, :]
    )
    return jnp.where(square > 0, (coulomb_scale / float(cells)) / jnp.maximum(square, 1.0), 0.0)


def band_shift(block, groups, distance):
    if distance % groups == 0:
        return block
    route = [((b + distance) % groups, b) for b in range(groups)]
    return lax.ppermute(block, "band", route)


def pencils(own, partners, groups, slabs):
    length = own.shape[3]
    own_count, part_count = own.shape[0], partners.shape[0]
    table = jnp.asarray(cas_table(length))
    rows_y = length // slabs
    waves = frequency(lax.iota(jnp.int32, length), length)
    y_waves = frequency(
        lax.axis_index("slab") * rows_y + lax.iota(jnp.int32, rows_y), length
    )
    kernel = coulomb(waves, y_waves, waves, length**3)
    own_acc = jnp.zeros(own.shape, jnp.float32)
    part_acc = jnp.zeros(partners.shape, jnp.float32)
    for step_no in sorted(range(1, STEPS + 1), key=lambda s: s % groups != 0):
        bands = band_shift(own, groups, step_no)
        field = (bands[:, None] * partners[None]).reshape((-1,) + own.shape[1:])
        field = apply_table("pzyx,xk->pzyk", field, table)
        field = apply_table("pzyx,yk->pzkx", field, table)
        field = lax.all_to_all(field, "slab", split_axis=2, concat_axis=1, tiled=True)
        field = apply_table("pzyx,zk->pkyx", field, table) * kernel
        field = apply_table("pzyx,zk->pkyx", field, table)
        field = lax.all_to_all(field, "slab", split_axis=1, concat_axis=2, tiled=True)
        field = apply_table("pzyx,yk->pzkx", field, table)
        field = apply_table("pzyx,xk->pzyk", field, table)
        potential = field.reshape((own_count, part_count) + own.shape[1:])
        part_acc = part_acc + jnp.sum(potential * bands[:, None], axis=0)
        own_add = jnp.sum(potential * partners[None], axis=1)
        own_acc = own_acc + band_shift(own_add, groups, -step_no)
    return own_acc, part_acc


def two_terms(values):
    high = values.astype(jnp.bfloat16)
    return high, (values - high.astype(jnp.float32)).astype(jnp.bfloat16)


def table_terms(length):
    table = cas_table(length)
    high = table.astype(ml_dtypes.bfloat16)
    low = (table - high.astype(np.float32)).astype(ml_dtypes.bfloat16)
    return high, low


def from_left(high, low, xp=np):
    return xp.concatenate([xp.concatenate([high, high], 1), xp.concatenate([low, low], 1)], 0)


def product(left, right):
    return jnp.dot(left, right, preferred_element_type=jnp.float32)


def along_x(rows, right):
    high, low = two_terms(rows)
    both = product(jnp.concatenate([high, low], 1), right)
    return both[:, : both.shape[1] // 2] + both[:, both.shape[1] // 2 :]


def along_y(columns, left):
    high, low = two_terms(columns)
    both = product(left, jnp.concatenate([high, low], 0))
    return both[: both.shape[0] // 2] + both[both.shape[0] // 2 :]


def slab_pieces(refs):
    first, first_x, second, second_x, parts, parts_c = refs
    return [(first, parts), (first_x, parts), (second, parts_c), (second_x, parts_c)]


def gather_kernel(right_ref, left_ref, *refs):
    pieces, out_ref, pair_ref = refs[:6], refs[6], refs[7]
    step = pl.program_id(0)
    rows, length = pair_ref.shape[0], pair_ref.shape[1]
    for turn, (own_ref, part_ref) in enumerate(slab_pieces(pieces)):

        @pl.when(step // 2 == turn)
        def _(own_ref=own_ref, part_ref=part_ref):
            pair_ref[...] = own_ref[0] * part_ref[0]

    flat_out = out_ref.reshape(rows * length, length)
    for r in range(0, rows, 2):
        block = along_x(pair_ref[pl.ds(r, 2)].reshape(2 * length, length), right_ref[...])
        block = along_y(jnp.concatenate([block[:length], block[length:]], 1), left_ref[...])
        flat_out[pl.ds(r, length, stride=rows), :] = block[:, :length]
        flat_out[pl.ds(r + 1, length, stride=rows), :] = block[:, length:]


def column_kernel(left_ref, back_ref, coulomb_ref, a_ref, b_ref, a_out, b_out):
    count, half, length = a_ref.shape
    for k in range(0, count, 2):
        block = jnp.concatenate(
            [
                jnp.concatenate([a_ref[k], b_ref[k]], 0),
                jnp.concatenate([a_ref[k + 1], b_ref[k + 1]], 0),
            ],
            1,
        )
        block = along_y(block, left_ref[...])
        block = block * jnp.concatenate([coulomb_ref[k], coulomb_ref[k + 1]], 1)
        block = along_y(block, back_ref[...])
        for j in range(2):
            piece = block[:, j * length : (j + 1) * length]
            a_out[k + j] = piece[:half]
            b_out[k + j] = piece[half:]


def scatter_kernel(right_ref, left_ref, field_ref, *refs):
    pieces, outs, pot_ref = refs[:6], refs[-7:-1], refs[-1]
    step = pl.program_id(0)
    rows, length = pot_ref.shape[0], pot_ref.shape[1]
    flat = field_ref.reshape(rows * length, length)
    for r in range(0, rows, 2):
        block = jnp.concatenate(
            [flat[pl.ds(r, length, stride=rows), :], flat[pl.ds(r + 1, length, stride=rows), :]], 1
        )
        block = along_y(block, left_ref[...])
        block = jnp.concatenate([block[:, :length], block[:, length:]], 0)
        pot_ref[pl.ds(r, 2)] = along_x(block, right_ref[...]).reshape(2, length, length)
    for turn, (piece, out) in enumerate(zip(slab_pieces(pieces), slab_pieces(outs))):

        @pl.when(step // 2 == turn)
        def _(piece=piece, out=out):
            out[0][0] = pot_ref[...] * piece[1][0]
            out[1][0] = pot_ref[...] * piece[0][0]


def piece_specs(rows, length, z_low):
    def own_spec(turn):
        return pl.BlockSpec(
            (1, rows, length, length),
            lambda i: (jnp.clip(i - 2 * turn, 0, 1) * 2 + z_low, 0, 0, 0),
        )

    def part_spec(core):
        return pl.BlockSpec(
            (1, rows, length, length), lambda i: (jnp.clip(i - 4 * core, 0, 3), 0, 0, 0)
        )

    return [own_spec(turn) for turn in range(4)] + [part_spec(core) for core in range(2)]


def fixed_spec(shape):
    return pl.BlockSpec(shape, lambda i: (0,) * len(shape))


def settings(megabytes):
    return pltpu.CompilerParams(
        dimension_semantics=("arbitrary",), vmem_limit_bytes=megabytes * 2**20
    )


def cost(length, fields, transforms):
    cells = length**3
    return pl.CostEstimate(
        flops=transforms * 8 * cells * length, bytes_accessed=4 * fields * cells, transcendentals=0
    )


def gather_half(right, left, pieces, z_low):
    rows, length = pieces[0].shape[1], pieces[0].shape[2]
    return pl.pallas_call(
        gather_kernel,
        grid=(8,),
        in_specs=[fixed_spec(right.shape), fixed_spec(left.shape)] + piece_specs(rows, length, z_low),
        out_specs=pl.BlockSpec((length, rows, length), lambda i: (0, i, 0)),
        out_shape=jax.ShapeDtypeStruct((length, 8 * rows, length), jnp.float32),
        scratch_shapes=[pltpu.VMEM((rows, length, length), jnp.float32)],
        compiler_params=settings(16),
        cost_estimate=cost(length, 2, 1),
    )(right, left, *pieces)


def columns(left, back, coulomb_table, a, b):
    length, half = a.shape[0], a.shape[1]
    count = 8
    block = pl.BlockSpec((count, half, length), lambda i: (i, 0, 0))
    return pl.pallas_call(
        column_kernel,
        grid=(length // count,),
        in_specs=[
            fixed_spec(left.shape), fixed_spec(back.shape),
            pl.BlockSpec((count, length, length), lambda i: (i, 0, 0)), block, block,
        ],
        out_specs=[block, block],
        out_shape=[jax.ShapeDtypeStruct(a.shape, jnp.float32)] * 2,
        compiler_params=settings(12),
        cost_estimate=cost(length, 3, 2),
    )(left, back, coulomb_table, a, b)


def scatter_half(right, left, field, pieces, z_low, held):
    rows, length = pieces[0].shape[1], pieces[0].shape[2]
    specs = piece_specs(rows, length, z_low)
    count = len(held)
    return pl.pallas_call(
        scatter_kernel,
        grid=(8,),
        in_specs=[
            fixed_spec(right.shape), fixed_spec(left.shape),
            pl.BlockSpec((length, rows, length), lambda i: (0, i, 0)),
        ]
        + specs
        + [pl.BlockSpec(memory_space=pl.ANY)] * count,
        out_specs=specs,
        out_shape=[jax.ShapeDtypeStruct(piece.shape, jnp.float32) for piece in pieces],
        input_output_aliases={9 + k: k for k in range(count)},
        scratch_shapes=[pltpu.VMEM((rows, length, length), jnp.float32)],
        compiler_params=settings(24),
        cost_estimate=cost(length, 3, 1),
    )(right, left, field, *pieces, *held)


def whole_fields(own, partners, groups, slabs):
    length = own.shape[3]
    rows = own.shape[1]
    plane = own.shape[2:]
    me = lax.axis_index("slab")
    part_half, own_band, part_low = (me >> 3) & 1, (me >> 2) & 1, (me >> 1) & 1

    at_home = ((me & 1) + 1) % groups == 0

    def swap(block, mask):
        return lax.ppermute(block, "slab", [(i ^ mask, i) for i in range(slabs)])

    def swap_away(block, mask):
        away = [i for i in range(slabs) if ((i & 1) + 1) % groups != 0]
        return lax.ppermute(block, "slab", [(i ^ mask, i) for i in away])

    def across(block, flip, back):
        route = []
        for b in range(groups):
            for i in range(slabs):
                source = ((b + 1 + (i & 1)) % groups) * slabs + (i ^ flip)
                target = b * slabs + i
                if source != target:
                    route.append((target, source) if back else (source, target))
        return lax.ppermute(block, ("band", "slab"), route)

    def pick(block, position, axis=0):
        return lax.dynamic_index_in_dim(block, position, axis, keepdims=False)

    def ordered(position, mine, other, axis=0):
        return jnp.where(
            position == 0, jnp.stack([mine, other], axis), jnp.stack([other, mine], axis)
        )

    def together(*blocks):
        return lax.optimization_barrier(blocks)

    high, low = table_terms(length)
    left = jnp.asarray(from_left(high, low))
    right = jnp.asarray(from_left(high, low).T)
    position = lax.iota(jnp.int32, slabs)
    slab_of = me ^ (
        (position & 1) * 8 + (position & 2) + (position & 4) // 4 + (position & 8) // 2
    )
    z_high, z_low = [
        jnp.take(jnp.asarray(term).reshape(slabs, rows, length), slab_of, axis=0).reshape(
            length, length
        )
        for term in (high, low)
    ]
    z_left, z_back = from_left(z_high.T, z_low.T, jnp), from_left(z_high, z_low, jnp)
    waves = frequency(lax.iota(jnp.int32, length), length)
    coulomb_table = coulomb(waves, waves, waves, length**3)

    kept, passed = pick(own, own_band), pick(own, 1 - own_band)
    bands = jnp.stack([kept, swap(passed, 4), swap(kept, 8), swap(passed, 12)])
    parts = partners.reshape((2, 2) + partners.shape[1:])
    parts = jnp.stack([pick(parts, part_low, 1), swap(pick(parts, 1 - part_low, 1), 2)])
    bands, parts = together(bands, parts)
    bands_x = swap(bands, 2)
    first, second = across(bands, 0, False), across(bands, 1, False)
    parts = jnp.stack([pick(parts, part_half, 1), swap(pick(parts, 1 - part_half, 1), 8)], 1)
    bands_x, first, second, parts = together(bands_x, first, second, parts)
    parts = parts.reshape((4, rows) + plane)
    parts_z, parts_c = swap(parts, 4), swap(parts, 1)
    first_x, second_x = swap_away(first, 2), across(bands_x, 1, False)
    first = jnp.where(at_home, bands, first)
    first_x = jnp.where(at_home, bands_x, first_x)
    own_pieces = [first, first_x, second, second_x]
    even = own_pieces + [parts, parts_c]
    field_even = gather_half(right, left, even, 0)
    parts_z, field_even = together(parts_z, field_even)
    odd = own_pieces + [parts_z, swap(parts_z, 1)]
    field_odd = gather_half(right, left, odd, 1)

    field_even, field_odd = columns(z_left, z_back, coulomb_table, field_even, field_odd)

    *own_pieces, parts_z, parts_zc = scatter_half(right, left, field_odd, odd, 1, [])
    parts_zc = swap(parts_zc, 1)
    *own_pieces, parts, parts_c = scatter_half(right, left, field_even, even, 0, own_pieces)
    *own_pieces, parts, parts_c, parts_z, parts_zc = together(
        *own_pieces, parts, parts_c, parts_z, parts_zc
    )
    parts_z = swap(parts_z + parts_zc, 4)
    first, first_x, second, second_x = own_pieces
    bands_x = across(second_x, 1, True) + jnp.where(at_home, first_x, 0.0)
    first = first + swap_away(first_x, 2)
    parts = (parts + swap(parts_c, 1) + parts_z).reshape((2, 2, rows) + plane)
    bands_x, first, second, parts = together(bands_x, first, second, parts)
    bands = across(first, 0, True) + across(second, 1, True) + swap(bands_x, 2)
    bands = bands + jnp.where(at_home, first, 0.0)
    parts = ordered(part_half, parts[:, 0], swap(parts[:, 1], 8), 1)
    bands, parts = together(bands, parts)
    kept = bands[0] + swap(bands[2], 8)
    passed = swap(bands[1], 4) + swap(bands[3], 12)
    parts = ordered(part_low, parts[0], swap(parts[1], 2), 1)
    return ordered(own_band, kept, passed), parts.reshape(partners.shape)


def solution(mesh):
    groups, slabs = mesh.shape["band"], mesh.shape["slab"]
    spec = P("band", "slab", None, None)

    def shards(own, partners):
        if slabs == 16 and own.shape[0] == 2 and partners.shape[0] == 4 and STEPS == 2:
            return whole_fields(own, partners, groups, slabs)
        return pencils(own, partners, groups, slabs)

    return jax.shard_map(
        shards, mesh=mesh, in_specs=(spec, spec), out_specs=(spec, spec), check_vma=False
    )
```

```python
import math

import jax
import jax.numpy as jnp
import ml_dtypes
import numpy as np
from jax import lax
from jax.experimental import pallas as pl
from jax.experimental.pallas import tpu as pltpu
from jax.sharding import PartitionSpec as P

STEPS = 2


coulomb_scale = 46.9 * 46.9 / math.pi
precision = lax.Precision.HIGH


def cas_table(length):
    half = length // 2
    angles = np.arange(half) * (2.0 * math.pi / length)
    first = (np.cos(angles) + np.sin(angles)).astype(np.float32)
    wave = np.concatenate([first, -first])
    positions = np.arange(length)
    return wave[(positions[:, None] * positions[None, :]) % length]


def apply_table(pattern, field, table):
    return jnp.einsum(pattern, field, table, precision=precision)


def frequency(positions, length):
    return jnp.where(positions < length // 2, positions, positions - length).astype(jnp.float32)


def coulomb(z_waves, y_waves, x_waves, cells):
    square = (
        z_waves[:, None, None] * z_waves[:, None, None]
        + y_waves[None, :, None] * y_waves[None, :, None]
        + x_waves[None, None, :] * x_waves[None, None, :]
    )
    return jnp.where(square > 0, (coulomb_scale / float(cells)) / jnp.maximum(square, 1.0), 0.0)


def band_shift(block, groups, distance):
    if distance % groups == 0:
        return block
    route = [((b + distance) % groups, b) for b in range(groups)]
    return lax.ppermute(block, "band", route)


def pencils(own, partners, groups, slabs):
    length = own.shape[3]
    own_count, part_count = own.shape[0], partners.shape[0]
    table = jnp.asarray(cas_table(length))
    rows_y = length // slabs
    waves = frequency(lax.iota(jnp.int32, length), length)
    y_waves = frequency(
        lax.axis_index("slab") * rows_y + lax.iota(jnp.int32, rows_y), length
    )
    kernel = coulomb(waves, y_waves, waves, length**3)
    own_acc = jnp.zeros(own.shape, jnp.float32)
    part_acc = jnp.zeros(partners.shape, jnp.float32)
    for step_no in sorted(range(1, STEPS + 1), key=lambda s: s % groups != 0):
        bands = band_shift(own, groups, step_no)
        field = (bands[:, None] * partners[None]).reshape((-1,) + own.shape[1:])
        field = apply_table("pzyx,xk->pzyk", field, table)
        field = apply_table("pzyx,yk->pzkx", field, table)
        field = lax.all_to_all(field, "slab", split_axis=2, concat_axis=1, tiled=True)
        field = apply_table("pzyx,zk->pkyx", field, table) * kernel
        field = apply_table("pzyx,zk->pkyx", field, table)
        field = lax.all_to_all(field, "slab", split_axis=1, concat_axis=2, tiled=True)
        field = apply_table("pzyx,yk->pzkx", field, table)
        field = apply_table("pzyx,xk->pzyk", field, table)
        potential = field.reshape((own_count, part_count) + own.shape[1:])
        part_acc = part_acc + jnp.sum(potential * bands[:, None], axis=0)
        own_add = jnp.sum(potential * partners[None], axis=1)
        own_acc = own_acc + band_shift(own_add, groups, -step_no)
    return own_acc, part_acc


def two_terms(values):
    high = values.astype(jnp.bfloat16)
    return high, (values - high.astype(jnp.float32)).astype(jnp.bfloat16)


def table_terms(length):
    table = cas_table(length)
    high = table.astype(ml_dtypes.bfloat16)
    low = (table - high.astype(np.float32)).astype(ml_dtypes.bfloat16)
    return high, low


def from_left(high, low, xp=np):
    return xp.concatenate([xp.concatenate([high, high], 1), xp.concatenate([low, low], 1)], 0)


def product(left, right):
    return jnp.dot(left, right, preferred_element_type=jnp.float32)


def along_x(rows, right):
    high, low = two_terms(rows)
    both = product(jnp.concatenate([high, low], 1), right)
    return both[:, : both.shape[1] // 2] + both[:, both.shape[1] // 2 :]


def along_y(columns, left):
    high, low = two_terms(columns)
    both = product(left, jnp.concatenate([high, low], 0))
    return both[: both.shape[0] // 2] + both[both.shape[0] // 2 :]


def slab_pieces(refs):
    own_refs, part_refs = refs[:4], refs[4:]
    return [(own_refs[i // 2], part_refs[i // 4 * 2 + i % 2]) for i in range(8)]


def gather_kernel(right_ref, left_ref, *refs):
    pieces, out_ref, pair_ref = refs[:8], refs[8], refs[9]
    step = pl.program_id(0)
    rows, length = pair_ref.shape[0], pair_ref.shape[1]
    for turn, (own_ref, part_ref) in enumerate(slab_pieces(pieces)):

        @pl.when(step == turn)
        def _(own_ref=own_ref, part_ref=part_ref):
            pair_ref[...] = own_ref[0] * part_ref[0]

    flat_out = out_ref.reshape(rows * length, length)
    for r in range(0, rows, 2):
        block = along_x(pair_ref[pl.ds(r, 2)].reshape(2 * length, length), right_ref[...])
        block = along_y(jnp.concatenate([block[:length], block[length:]], 1), left_ref[...])
        flat_out[pl.ds(r, length, stride=rows), :] = block[:, :length]
        flat_out[pl.ds(r + 1, length, stride=rows), :] = block[:, length:]


def column_kernel(left_ref, back_ref, coulomb_ref, a_ref, b_ref, a_out, b_out):
    count, half, length = a_ref.shape
    for k in range(0, count, 2):
        block = jnp.concatenate(
            [
                jnp.concatenate([a_ref[k], b_ref[k]], 0),
                jnp.concatenate([a_ref[k + 1], b_ref[k + 1]], 0),
            ],
            1,
        )
        block = along_y(block, left_ref[...])
        block = block * jnp.concatenate([coulomb_ref[k], coulomb_ref[k + 1]], 1)
        block = along_y(block, back_ref[...])
        for j in range(2):
            piece = block[:, j * length : (j + 1) * length]
            a_out[k + j] = piece[:half]
            b_out[k + j] = piece[half:]


def scatter_kernel(right_ref, left_ref, field_ref, *refs):
    pieces, outs, pot_ref = refs[:8], refs[-9:-1], refs[-1]
    step = pl.program_id(0)
    rows, length = pot_ref.shape[0], pot_ref.shape[1]
    flat = field_ref.reshape(rows * length, length)
    for r in range(0, rows, 2):
        block = jnp.concatenate(
            [flat[pl.ds(r, length, stride=rows), :], flat[pl.ds(r + 1, length, stride=rows), :]], 1
        )
        block = along_y(block, left_ref[...])
        block = jnp.concatenate([block[:, :length], block[:, length:]], 0)
        pot_ref[pl.ds(r, 2)] = along_x(block, right_ref[...]).reshape(2, length, length)
    for turn, (piece, out) in enumerate(zip(slab_pieces(pieces), slab_pieces(outs))):

        @pl.when(step == turn)
        def _(piece=piece, out=out):
            out[0][0] = pot_ref[...] * piece[1][0]
            out[1][0] = pot_ref[...] * piece[0][0]


def piece_specs(rows, length, z_low):
    def own_spec(turn):
        return pl.BlockSpec(
            (1, rows, length, length),
            lambda i: (jnp.clip(i - 2 * turn, 0, 1) * 2 + z_low, 0, 0, 0),
        )

    def part_spec(core, z_high):
        return pl.BlockSpec(
            (1, rows, length, length),
            lambda i: (jnp.where(i >= 4 * core + z_high + 2, 1, 0), 0, 0, 0),
        )

    return [own_spec(turn) for turn in range(4)] + [part_spec(k // 2, k % 2) for k in range(4)]


def fixed_spec(shape):
    return pl.BlockSpec(shape, lambda i: (0,) * len(shape))


def settings(megabytes):
    return pltpu.CompilerParams(
        dimension_semantics=("arbitrary",), vmem_limit_bytes=megabytes * 2**20
    )


def cost(length, fields, transforms):
    cells = length**3
    return pl.CostEstimate(
        flops=transforms * 8 * cells * length, bytes_accessed=4 * fields * cells, transcendentals=0
    )


def gather_half(right, left, pieces, z_low):
    rows, length = pieces[0].shape[1], pieces[0].shape[2]
    return pl.pallas_call(
        gather_kernel,
        grid=(8,),
        in_specs=[fixed_spec(right.shape), fixed_spec(left.shape)] + piece_specs(rows, length, z_low),
        out_specs=pl.BlockSpec((length, rows, length), lambda i: (0, i, 0)),
        out_shape=jax.ShapeDtypeStruct((length, 8 * rows, length), jnp.float32),
        scratch_shapes=[pltpu.VMEM((rows, length, length), jnp.float32)],
        compiler_params=settings(16),
        cost_estimate=cost(length, 2, 1),
    )(right, left, *pieces)


def columns(left, back, coulomb_table, a, b):
    length, half = a.shape[0], a.shape[1]
    count = 8
    block = pl.BlockSpec((count, half, length), lambda i: (i, 0, 0))
    return pl.pallas_call(
        column_kernel,
        grid=(length // count,),
        in_specs=[
            fixed_spec(left.shape), fixed_spec(back.shape),
            pl.BlockSpec((count, length, length), lambda i: (i, 0, 0)), block, block,
        ],
        out_specs=[block, block],
        out_shape=[jax.ShapeDtypeStruct(a.shape, jnp.float32)] * 2,
        compiler_params=settings(12),
        cost_estimate=cost(length, 3, 2),
    )(left, back, coulomb_table, a, b)


def scatter_half(right, left, field, pieces, z_low, held):
    rows, length = pieces[0].shape[1], pieces[0].shape[2]
    specs = piece_specs(rows, length, z_low)
    count = len(held)
    return pl.pallas_call(
        scatter_kernel,
        grid=(8,),
        in_specs=[
            fixed_spec(right.shape), fixed_spec(left.shape),
            pl.BlockSpec((length, rows, length), lambda i: (0, i, 0)),
        ]
        + specs
        + [pl.BlockSpec(memory_space=pl.ANY)] * count,
        out_specs=specs,
        out_shape=[jax.ShapeDtypeStruct(piece.shape, jnp.float32) for piece in pieces],
        input_output_aliases={11 + k: k for k in range(count)},
        scratch_shapes=[pltpu.VMEM((rows, length, length), jnp.float32)],
        compiler_params=settings(24),
        cost_estimate=cost(length, 3, 1),
    )(right, left, field, *pieces, *held)


def whole_fields(own, partners, groups, slabs):
    length = own.shape[3]
    rows = own.shape[1]
    plane = own.shape[2:]
    me = lax.axis_index("slab")
    part_half, own_band, part_low = (me >> 3) & 1, (me >> 2) & 1, (me >> 1) & 1

    at_home = ((me & 1) + 1) % groups == 0

    def swap(block, mask):
        return lax.ppermute(block, "slab", [(i ^ mask, i) for i in range(slabs)])

    def swap_away(block, mask):
        away = [i for i in range(slabs) if ((i & 1) + 1) % groups != 0]
        return lax.ppermute(block, "slab", [(i ^ mask, i) for i in away])

    def across(block, flip, back):
        route = []
        for b in range(groups):
            for i in range(slabs):
                source = ((b + 1 + (i & 1)) % groups) * slabs + (i ^ flip)
                target = b * slabs + i
                if source != target:
                    route.append((target, source) if back else (source, target))
        return lax.ppermute(block, ("band", "slab"), route)

    def pick(block, position, axis=0):
        return lax.dynamic_index_in_dim(block, position, axis, keepdims=False)

    def ordered(position, mine, other, axis=0):
        return jnp.where(
            position == 0, jnp.stack([mine, other], axis), jnp.stack([other, mine], axis)
        )

    def together(*blocks):
        return lax.optimization_barrier(blocks)

    high, low = table_terms(length)
    left = jnp.asarray(from_left(high, low))
    right = jnp.asarray(from_left(high, low).T)
    position = lax.iota(jnp.int32, slabs)
    slab_of = me ^ (
        (position & 1) * 8 + (position & 2) + (position & 4) // 4 + (position & 8) // 2
    )
    z_high, z_low = [
        jnp.take(jnp.asarray(term).reshape(slabs, rows, length), slab_of, axis=0).reshape(
            length, length
        )
        for term in (high, low)
    ]
    z_left, z_back = from_left(z_high.T, z_low.T, jnp), from_left(z_high, z_low, jnp)
    waves = frequency(lax.iota(jnp.int32, length), length)
    coulomb_table = coulomb(waves, waves, waves, length**3)

    kept, passed = pick(own, own_band), pick(own, 1 - own_band)
    from_z = [swap(kept, 8), swap(passed, 12), swap(passed, 4)]
    parts = partners.reshape((2, 2) + partners.shape[1:])
    parts, parts_x = pick(parts, part_low, 1), swap(pick(parts, 1 - part_low, 1), 2)
    kept_near = jnp.stack([pick(parts, part_half), pick(parts_x, part_half)])
    leaving = jnp.stack([pick(parts, 1 - part_half), pick(parts_x, 1 - part_half)])
    kept_near, leaving, *from_z = together(kept_near, leaving, *from_z)
    got_near, kept_far = swap(leaving, 8), swap(kept_near, 4)
    bands = jnp.stack([kept, from_z[2], from_z[0], from_z[1]])
    bands_x = swap(bands, 2)
    first, second = across(bands, 0, False), across(bands, 1, False)
    bands_x, first, second, got_near, kept_far = together(
        bands_x, first, second, got_near, kept_far
    )
    got_far = swap(got_near, 4)
    first_x, second_x = swap_away(first, 2), across(bands_x, 1, False)
    near = [kept_near, got_near, swap(kept_near, 1), swap(got_near, 1)]
    kept_far_c = swap(kept_far, 1)
    first = jnp.where(at_home, bands, first)
    first_x = jnp.where(at_home, bands_x, first_x)
    own_pieces = [first, first_x, second, second_x]
    field_near = gather_half(right, left, own_pieces + near, 0)
    far = [kept_far, got_far, kept_far_c, swap(got_far, 1)]
    field_far = gather_half(right, left, own_pieces + far, 1)

    field_near, field_far = columns(z_left, z_back, coulomb_table, field_near, field_far)

    outs = scatter_half(right, left, field_far, own_pieces + far, 1, [])
    kept_far_c, got_far_c = swap(outs[6], 1), swap(outs[7], 1)
    kept_far, got_far = outs[4], outs[5]
    outs = scatter_half(right, left, field_near, own_pieces + near, 0, outs[:4])
    *outs, kept_far, got_far, kept_far_c, got_far_c = together(
        *outs, kept_far, got_far, kept_far_c, got_far_c
    )
    got_near = swap(got_far + got_far_c, 4)
    first, first_x, second, second_x = outs[:4]
    bands_x = across(second_x, 1, True) + jnp.where(at_home, first_x, 0.0)
    first = first + swap_away(first_x, 2)
    kept_far = kept_far + kept_far_c
    kept_near = outs[4] + swap(outs[6], 1)
    got_near = got_near + outs[5] + swap(outs[7], 1)
    bands_x, first, second, kept_far, kept_near, got_near = together(
        bands_x, first, second, kept_far, kept_near, got_near
    )
    leaving = swap(got_near, 8)
    kept_near = kept_near + swap(kept_far, 4)
    bands = across(first, 0, True) + across(second, 1, True) + swap(bands_x, 2)
    bands = bands + jnp.where(at_home, first, 0.0)
    bands, kept_near, leaving = together(bands, kept_near, leaving)
    kept = bands[0] + swap(bands[2], 8)
    passed = swap(bands[1], 4) + swap(bands[3], 12)
    parts_x = swap(ordered(part_half, kept_near[1], leaving[1]), 2)
    parts = ordered(part_low, ordered(part_half, kept_near[0], leaving[0]), parts_x, 1)
    return ordered(own_band, kept, passed), parts.reshape(partners.shape)


def solution(mesh):
    groups, slabs = mesh.shape["band"], mesh.shape["slab"]
    spec = P("band", "slab", None, None)

    def shards(own, partners):
        if slabs == 16 and own.shape[0] == 2 and partners.shape[0] == 4 and STEPS == 2:
            return whole_fields(own, partners, groups, slabs)
        return pencils(own, partners, groups, slabs)

    return jax.shard_map(
        shards, mesh=mesh, in_specs=(spec, spec), out_specs=(spec, spec), check_vma=False
    )
```

```python
import functools
import math

import jax
import jax.numpy as jnp
import ml_dtypes
import numpy as np
from jax import lax
from jax.experimental import pallas as pl
from jax.experimental.pallas import tpu as pltpu
from jax.sharding import PartitionSpec as P

STEPS = 2


coulomb_scale = 46.9 * 46.9 / math.pi
precision = lax.Precision.HIGH


def cas_table(length):
    half = length // 2
    angles = np.arange(half) * (2.0 * math.pi / length)
    first = (np.cos(angles) + np.sin(angles)).astype(np.float32)
    wave = np.concatenate([first, -first])
    positions = np.arange(length)
    return wave[(positions[:, None] * positions[None, :]) % length]


def apply_table(pattern, field, table):
    return jnp.einsum(pattern, field, table, precision=precision)


def frequency(positions, length):
    return jnp.where(positions < length // 2, positions, positions - length).astype(jnp.float32)


def coulomb(z_waves, y_waves, x_waves, cells):
    square = (
        z_waves[:, None, None] * z_waves[:, None, None]
        + y_waves[None, :, None] * y_waves[None, :, None]
        + x_waves[None, None, :] * x_waves[None, None, :]
    )
    return jnp.where(square > 0, (coulomb_scale / float(cells)) / jnp.maximum(square, 1.0), 0.0)


def band_shift(block, groups, distance):
    if distance % groups == 0:
        return block
    route = [((b + distance) % groups, b) for b in range(groups)]
    return lax.ppermute(block, "band", route)


def pencils(own, partners, groups, slabs):
    length = own.shape[3]
    own_count, part_count = own.shape[0], partners.shape[0]
    table = jnp.asarray(cas_table(length))
    rows_y = length // slabs
    waves = frequency(lax.iota(jnp.int32, length), length)
    y_waves = frequency(
        lax.axis_index("slab") * rows_y + lax.iota(jnp.int32, rows_y), length
    )
    kernel = coulomb(waves, y_waves, waves, length**3)
    own_acc = jnp.zeros(own.shape, jnp.float32)
    part_acc = jnp.zeros(partners.shape, jnp.float32)
    for step_no in sorted(range(1, STEPS + 1), key=lambda s: s % groups != 0):
        bands = band_shift(own, groups, step_no)
        field = (bands[:, None] * partners[None]).reshape((-1,) + own.shape[1:])
        field = apply_table("pzyx,xk->pzyk", field, table)
        field = apply_table("pzyx,yk->pzkx", field, table)
        field = lax.all_to_all(field, "slab", split_axis=2, concat_axis=1, tiled=True)
        field = apply_table("pzyx,zk->pkyx", field, table) * kernel
        field = apply_table("pzyx,zk->pkyx", field, table)
        field = lax.all_to_all(field, "slab", split_axis=1, concat_axis=2, tiled=True)
        field = apply_table("pzyx,yk->pzkx", field, table)
        field = apply_table("pzyx,xk->pzyk", field, table)
        potential = field.reshape((own_count, part_count) + own.shape[1:])
        part_acc = part_acc + jnp.sum(potential * bands[:, None], axis=0)
        own_add = jnp.sum(potential * partners[None], axis=1)
        own_acc = own_acc + band_shift(own_add, groups, -step_no)
    return own_acc, part_acc


def two_terms(values):
    high = values.astype(jnp.bfloat16)
    return high, (values - high.astype(jnp.float32)).astype(jnp.bfloat16)


def table_terms(length):
    table = cas_table(length)
    high = table.astype(ml_dtypes.bfloat16)
    low = (table - high.astype(np.float32)).astype(ml_dtypes.bfloat16)
    return high, low


def from_left(high, low, xp=np):
    return xp.concatenate([xp.concatenate([high, high], 1), xp.concatenate([low, low], 1)], 0)


def product(left, right):
    return jnp.dot(left, right, preferred_element_type=jnp.float32)


def along_x(rows, right):
    high, low = two_terms(rows)
    both = product(jnp.concatenate([high, low], 1), right)
    return both[:, : both.shape[1] // 2] + both[:, both.shape[1] // 2 :]


def along_y(columns, left):
    high, low = two_terms(columns)
    both = product(left, jnp.concatenate([high, low], 0))
    return both[: both.shape[0] // 2] + both[both.shape[0] // 2 :]


def steps_of(late):
    steps = []
    for core in range(2):
        for x, z in [(1, 0), (1, 1), (1, 2), (0, 3), (1, 3)] if late else [(0, 0), (0, 1), (0, 2)]:
            steps.append((2 * core + x, z, 4 + 4 * core + z, x))
    return steps


EARLY, LATE = steps_of(False), steps_of(True)


def slabs_of(steps):
    return [(z >> 1) * 8 + (z & 1) * 4 + x * 2 + own // 2 for own, z, part, x in steps]


def used(steps):
    return sorted({step[0] for step in steps} | {step[2] for step in steps})


def to_field(pair_ref, out_ref, right, left):
    rows, length = pair_ref.shape[0], pair_ref.shape[1]
    for r in range(0, rows, 2):
        block = along_x(pair_ref[pl.ds(r, 2)].reshape(2 * length, length), right)
        block = along_y(jnp.concatenate([block[:length], block[length:]], 1), left)
        out_ref[pl.ds(r, length, stride=rows), :] = block[:, :length]
        out_ref[pl.ds(r + 1, length, stride=rows), :] = block[:, length:]


def from_field(field_ref, pot_ref, right, left):
    rows, length = pot_ref.shape[0], pot_ref.shape[1]
    for r in range(0, rows, 2):
        block = jnp.concatenate(
            [field_ref[pl.ds(r + k, length, stride=rows), :] for k in range(2)], 1
        )
        block = along_y(block, left)
        block = jnp.concatenate([block[:, :length], block[:, length:]], 0)
        pot_ref[pl.ds(r, 2)] = along_x(block, right).reshape(2, length, length)


def make_pairs(steps, turn, pieces, pair_ref):
    for k, (own, _, part, _) in enumerate(steps):

        @pl.when(turn == k)
        def _(own=own, part=part):
            pair_ref[...] = pieces[own][0] * pieces[part][0]


def make_terms(steps, turn, pieces, outs, pot_ref):
    for k, (own, _, part, _) in enumerate(steps):

        @pl.when(turn == k)
        def _(own=own, part=part):
            outs[own][0] = pot_ref[...] * pieces[part][0]
            outs[part][0] = pot_ref[...] * pieces[own][0]


def gather_kernel(steps, right_ref, left_ref, *refs):
    pieces, out_ref, pair_ref = dict(zip(used(steps), refs)), refs[-2], refs[-1]
    make_pairs(steps, pl.program_id(0), pieces, pair_ref)
    rows, length = pair_ref.shape[0], pair_ref.shape[1]
    to_field(pair_ref, out_ref.reshape(rows * length, length), right_ref[...], left_ref[...])


def late_kernel(
    steps, right_ref, left_ref, z_left_ref, z_back_ref, square_ref, early_ref, *refs
):
    names = used(steps)
    pieces, early_out = dict(zip(names, refs)), refs[len(names)]
    outs = dict(zip(names, refs[len(names) + 1 :]))
    own_ref, part_ref, field_ref, middle_ref, in_sems, out_sems, middle_sems = refs[-7:]
    rows, length = own_ref.shape[1], own_ref.shape[2]
    count, part = len(steps), middle_ref.shape[1]

    def blocks(k, arrays):
        own, z, part, x = steps[k]
        return [(arrays[own].at[z], own_ref.at[k]), (arrays[part].at[x], part_ref.at[k])]

    for k in range(count):
        for j, (block, held) in enumerate(blocks(k, pieces)):
            pltpu.make_async_copy(block, held, in_sems.at[j, k]).start()
    middle_in = pltpu.make_async_copy(early_ref, middle_ref, middle_sems.at[0])
    middle_in.start()

    @pl.loop(0, count)
    def _(k):
        pltpu.make_async_copy(pieces[names[0]].at[0], own_ref.at[k], in_sems.at[0, k]).wait()
        pltpu.make_async_copy(pieces[names[0]].at[0], part_ref.at[k], in_sems.at[1, k]).wait()
        out_ref = field_ref.at[k]
        for r in range(0, rows, 2):
            pair = own_ref[k, pl.ds(r, 2)] * part_ref[k, pl.ds(r, 2)]
            block = along_x(pair.reshape(2 * length, length), right_ref[...])
            block = along_y(
                jnp.concatenate([block[:length], block[length:]], 1), left_ref[...]
            )
            out_ref[pl.ds(r, length, stride=rows), :] = block[:, :length]
            out_ref[pl.ds(r + 1, length, stride=rows), :] = block[:, length:]

    middle_in.wait()
    group = 8
    scale = coulomb_scale / float(length**3)

    @pl.loop(0, length // group)
    def _(i):
        for k in range(0, group, 2):
            columns, factors, spans = [], [], []
            for j in range(2):
                y = i * group + k + j
                spans.append(pl.ds(pl.multiple_of(y * rows, rows), rows))
                late = field_ref[:, spans[j], :].reshape(count * rows, length)
                columns.append(jnp.concatenate([middle_ref[y], late], 0))
                wave = frequency(y, length)
                total = square_ref[...] + wave * wave
                factors.append(jnp.where(total > 0, scale / jnp.maximum(total, 1.0), 0.0))
            block = along_y(jnp.concatenate(columns, 1), z_left_ref[...])
            block = along_y(block * jnp.concatenate(factors, 1), z_back_ref[...])
            for j in range(2):
                piece = block[:, j * length : (j + 1) * length]
                middle_ref[i * group + k + j] = piece[:part]
                field_ref[:, spans[j], :] = piece[part:].reshape(count, rows, length)

    middle_out = pltpu.make_async_copy(middle_ref, early_out, middle_sems.at[1])
    middle_out.start()

    @pl.loop(0, count)
    def _(k):
        in_ref = field_ref.at[k]
        for r in range(0, rows, 2):
            block = jnp.concatenate(
                [in_ref[pl.ds(r + j, length, stride=rows), :] for j in range(2)], 1
            )
            block = along_y(block, left_ref[...])
            block = jnp.concatenate([block[:, :length], block[:, length:]], 0)
            block = along_x(block, right_ref[...]).reshape(2, length, length)
            span = pl.ds(r, 2)
            own_term = block * part_ref[k, span]
            part_ref[k, span] = block * own_ref[k, span]
            own_ref[k, span] = own_term
        for turn in range(count):

            @pl.when(k == turn)
            def _(turn=turn):
                for j, (block, held) in enumerate(blocks(turn, outs)):
                    pltpu.make_async_copy(held, block, out_sems.at[j, turn]).start()

    for k in range(count):
        for j, (block, held) in enumerate(blocks(k, outs)):
            pltpu.make_async_copy(held, block, out_sems.at[j, k]).wait()
    middle_out.wait()


def scatter_kernel(steps, right_ref, left_ref, field_ref, *refs):
    names = used(steps)
    pieces, outs = dict(zip(names, refs)), dict(zip(names, refs[-1 - len(names) : -1]))
    pot_ref = refs[-1]
    rows, length = pot_ref.shape[0], pot_ref.shape[1]
    flat = field_ref.reshape(rows * length, length)
    from_field(flat, pot_ref, right_ref[...], left_ref[...])
    make_terms(steps, pl.program_id(0), pieces, outs, pot_ref)


def piece_specs(steps, rows, length, starts=(0,)):
    def spec(name):
        visits = []
        for start in starts:
            for turn, (own, z, part, x) in enumerate(steps):
                if name in (own, part):
                    visits.append((start + turn, z if name == own else x))

        def index(i):
            block = visits[0][1]
            for (_, before), (turn, after) in zip(visits, visits[1:]):
                block = block + jnp.where(i >= turn, after - before, 0)
            return (block, 0, 0, 0)

        return pl.BlockSpec((1, rows, length, length), index)

    return [spec(name) for name in used(steps)]


def fixed_spec(shape):
    return pl.BlockSpec(shape, lambda i: (0,) * len(shape))


def settings(megabytes):
    return pltpu.CompilerParams(
        dimension_semantics=("arbitrary",), vmem_limit_bytes=megabytes * 2**20
    )


def cost(cells, length, fields, transforms):
    return pl.CostEstimate(
        flops=transforms * 8 * cells * length, bytes_accessed=4 * fields * cells, transcendentals=0
    )


def gather_part(right, left, pieces, steps):
    rows, length = pieces[0].shape[1], pieces[0].shape[2]
    count = len(steps)
    return pl.pallas_call(
        functools.partial(gather_kernel, steps),
        grid=(count,),
        in_specs=[fixed_spec(right.shape), fixed_spec(left.shape)]
        + piece_specs(steps, rows, length),
        out_specs=pl.BlockSpec((length, rows, length), lambda i: (0, i, 0)),
        out_shape=jax.ShapeDtypeStruct((length, count * rows, length), jnp.float32),
        scratch_shapes=[pltpu.VMEM((rows, length, length), jnp.float32)],
        compiler_params=settings(20),
        cost_estimate=cost(count * rows * length * length, length, 3, 2),
    )(right, left, *[pieces[name] for name in used(steps)])


def late_part(right, left, z_left, z_back, square, early, pieces, steps):
    rows, length = pieces[0].shape[1], pieces[0].shape[2]
    names = used(steps)
    count = len(steps)
    tables = [right, left, z_left, z_back, square]
    anywhere = pl.BlockSpec(memory_space=pl.ANY)
    early, *outs = pl.pallas_call(
        functools.partial(late_kernel, steps),
        in_specs=[pl.BlockSpec(memory_space=pltpu.VMEM)] * len(tables)
        + [anywhere] * (1 + len(names)),
        out_specs=[anywhere] * (1 + len(names)),
        out_shape=[jax.ShapeDtypeStruct(early.shape, jnp.float32)]
        + [jax.ShapeDtypeStruct(pieces[name].shape, jnp.float32) for name in names],
        scratch_shapes=[
            pltpu.VMEM((count, rows, length, length), jnp.float32),
            pltpu.VMEM((count, rows, length, length), jnp.float32),
            pltpu.VMEM((count, rows * length, length), jnp.float32),
            pltpu.VMEM(early.shape, jnp.float32),
            pltpu.SemaphoreType.DMA((2, count)),
            pltpu.SemaphoreType.DMA((2, count)),
            pltpu.SemaphoreType.DMA((2,)),
        ],
        compiler_params=pltpu.CompilerParams(vmem_limit_bytes=32 * 2**20),
        cost_estimate=cost(length**3, length, 4, 5),
    )(*tables, early, *[pieces[name] for name in names])
    return early, dict(zip(names, outs))


def scatter_part(right, left, field, pieces, steps, held):
    rows, length = pieces[0].shape[1], pieces[0].shape[2]
    names = used(steps)
    specs = piece_specs(steps, rows, length)
    kept = [name for name in names if name in held]
    outs = pl.pallas_call(
        functools.partial(scatter_kernel, steps),
        grid=(len(steps),),
        in_specs=[
            fixed_spec(right.shape), fixed_spec(left.shape),
            pl.BlockSpec((length, rows, length), lambda i: (0, i, 0)),
        ]
        + specs
        + [pl.BlockSpec(memory_space=pl.ANY)] * len(kept),
        out_specs=specs,
        out_shape=[jax.ShapeDtypeStruct(pieces[name].shape, jnp.float32) for name in names],
        input_output_aliases={
            3 + len(names) + k: names.index(name) for k, name in enumerate(kept)
        },
        scratch_shapes=[pltpu.VMEM((rows, length, length), jnp.float32)],
        compiler_params=settings(32),
        cost_estimate=cost(len(steps) * rows * length * length, length, 5, 2),
    )(right, left, field, *[pieces[name] for name in names], *[held[name] for name in kept])
    return dict(zip(names, outs))


def whole_fields(own, partners, groups, slabs):
    length = own.shape[3]
    rows = own.shape[1]
    plane = own.shape[2:]
    me = lax.axis_index("slab")
    part_half, own_band, part_low = (me >> 3) & 1, (me >> 2) & 1, (me >> 1) & 1

    at_home = ((me & 1) + 1) % groups == 0

    def swap(block, mask):
        return lax.ppermute(block, "slab", [(i ^ mask, i) for i in range(slabs)])

    def swap_away(block, mask):
        away = [i for i in range(slabs) if ((i & 1) + 1) % groups != 0]
        return lax.ppermute(block, "slab", [(i ^ mask, i) for i in away])

    def across(block, flip, back):
        route = []
        for b in range(groups):
            for i in range(slabs):
                source = ((b + 1 + (i & 1)) % groups) * slabs + (i ^ flip)
                target = b * slabs + i
                if source != target:
                    route.append((target, source) if back else (source, target))
        return lax.ppermute(block, ("band", "slab"), route)

    def pick(block, position, axis=0):
        return lax.dynamic_index_in_dim(block, position, axis, keepdims=False)

    def ordered(position, mine, other, axis=0):
        shape = [1] * (mine.ndim + 1)
        shape[axis] = 2
        first = lax.iota(jnp.int32, 2).reshape(shape) == position
        return jnp.where(first, jnp.expand_dims(mine, axis), jnp.expand_dims(other, axis))

    def together(*blocks):
        return lax.optimization_barrier(blocks)

    high, low = table_terms(length)
    left = jnp.asarray(from_left(high, low))
    right = jnp.asarray(from_left(high, low).T)
    slab_of = me ^ jnp.asarray(np.array(slabs_of(EARLY) + slabs_of(LATE), np.int32))
    z_high, z_low = [
        jnp.take(jnp.asarray(term).reshape(slabs, rows, length), slab_of, axis=0).reshape(
            length, length
        )
        for term in (high, low)
    ]
    z_left, z_back = from_left(z_high.T, z_low.T, jnp), from_left(z_high, z_low, jnp)
    waves = frequency(lax.iota(jnp.int32, length), length)
    square = waves[:, None] * waves[:, None] + waves[None] * waves[None]

    kept, passed = pick(own, own_band), pick(own, 1 - own_band)
    from_z = [swap(kept, 8), swap(passed, 12), swap(passed, 4)]
    parts = partners.reshape((2, 2) + partners.shape[1:])
    parts, parts_x = pick(parts, part_low, 1), swap(pick(parts, 1 - part_low, 1), 2)
    kept_near = jnp.stack([pick(parts, part_half), pick(parts_x, part_half)])
    leaving = jnp.stack([pick(parts, 1 - part_half), pick(parts_x, 1 - part_half)])
    kept_near, leaving, *from_z = together(kept_near, leaving, *from_z)
    got_near, kept_far = swap(leaving, 8), swap(kept_near, 4)
    bands = jnp.stack([kept, from_z[2], from_z[0], from_z[1]])
    bands_x = swap(bands, 2)
    first, second = across(bands, 0, False), across(bands, 1, False)
    bands_x, first, second, got_near, kept_far = together(
        bands_x, first, second, got_near, kept_far
    )
    got_far = swap(got_near, 4)
    first_x, second_x = swap_away(first, 2), across(bands_x, 1, False)
    parts = [kept_near, kept_far, got_near]
    parts_c = [swap(part, 1) for part in parts]
    first = jnp.where(at_home, bands, first)
    early = [first, None, second, None] + parts + [None] + parts_c + [None]
    field_early = gather_part(right, left, early, EARLY)
    got_far, first_x, second_x, field_early = together(got_far, first_x, second_x, field_early)
    first_x = jnp.where(at_home, bands_x, first_x)
    pieces = [first, first_x, second, second_x] + parts + [got_far] + parts_c + [swap(got_far, 1)]
    field_early, outs = late_part(
        right, left, z_left, z_back, square, field_early, pieces, LATE
    )
    got_far = outs[7] + swap(outs[11], 1)
    got_far, field_early = together(got_far, field_early)
    got_near = swap(got_far, 4)
    first = swap_away(outs[1], 2)
    bands_x = across(outs[3], 1, True) + jnp.where(at_home, outs[1], 0.0)
    outs = scatter_part(right, left, field_early, pieces, EARLY, outs)
    names = sorted(outs)
    got_near, first, bands_x, *blocks = together(
        got_near, first, bands_x, *[outs[name] for name in names]
    )
    outs = dict(zip(names, blocks))
    got_near = got_near + outs[6] + swap(outs[10], 1)
    kept_far = outs[5] + swap(outs[9], 1)
    kept_near = outs[4] + swap(outs[8], 1)
    first, second = outs[0] + first, outs[2]
    leaving = swap(got_near, 8)
    kept_near = kept_near + swap(kept_far, 4)
    terms = [across(first, 0, True), across(second, 1, True), swap(bands_x, 2)]
    terms.append(jnp.where(at_home, first, 0.0))
    kept_near, leaving, *terms = together(kept_near, leaving, *terms)
    bands = [sum(term[z] for term in terms) for z in range(4)]
    parts_x = swap(ordered(part_half, kept_near[1], leaving[1]), 2)
    from_z = [swap(bands[2], 8), swap(bands[3], 12), swap(bands[1], 4)]
    parts = ordered(part_low, ordered(part_half, kept_near[0], leaving[0]), parts_x, 1)
    parts, *from_z = together(parts.reshape(partners.shape), *from_z)
    return ordered(own_band, bands[0] + from_z[0], from_z[1] + from_z[2]), parts


def solution(mesh):
    groups, slabs = mesh.shape["band"], mesh.shape["slab"]
    spec = P("band", "slab", None, None)

    def shards(own, partners):
        if slabs == 16 and own.shape[0] == 2 and partners.shape[0] == 4 and STEPS == 2:
            return whole_fields(own, partners, groups, slabs)
        return pencils(own, partners, groups, slabs)

    return jax.shard_map(
        shards, mesh=mesh, in_specs=(spec, spec), out_specs=(spec, spec), check_vma=False
    )
```

```python
import functools
import math

import jax
import jax.numpy as jnp
import ml_dtypes
import numpy as np
from jax import lax
from jax.experimental import pallas as pl
from jax.experimental.pallas import tpu as pltpu
from jax.sharding import PartitionSpec as P

STEPS = 2


coulomb_scale = 46.9 * 46.9 / math.pi
precision = lax.Precision.HIGH


def cas_table(length):
    half = length // 2
    angles = np.arange(half) * (2.0 * math.pi / length)
    first = (np.cos(angles) + np.sin(angles)).astype(np.float32)
    wave = np.concatenate([first, -first])
    positions = np.arange(length)
    return wave[(positions[:, None] * positions[None, :]) % length]


def apply_table(pattern, field, table):
    return jnp.einsum(pattern, field, table, precision=precision)


def frequency(positions, length):
    return jnp.where(positions < length // 2, positions, positions - length).astype(jnp.float32)


def coulomb(z_waves, y_waves, x_waves, cells):
    square = (
        z_waves[:, None, None] * z_waves[:, None, None]
        + y_waves[None, :, None] * y_waves[None, :, None]
        + x_waves[None, None, :] * x_waves[None, None, :]
    )
    return jnp.where(square > 0, (coulomb_scale / float(cells)) / jnp.maximum(square, 1.0), 0.0)


def band_shift(block, groups, distance):
    if distance % groups == 0:
        return block
    route = [((b + distance) % groups, b) for b in range(groups)]
    return lax.ppermute(block, "band", route)


def pencils(own, partners, groups, slabs):
    length = own.shape[3]
    own_count, part_count = own.shape[0], partners.shape[0]
    table = jnp.asarray(cas_table(length))
    rows_y = length // slabs
    waves = frequency(lax.iota(jnp.int32, length), length)
    y_waves = frequency(
        lax.axis_index("slab") * rows_y + lax.iota(jnp.int32, rows_y), length
    )
    kernel = coulomb(waves, y_waves, waves, length**3)
    own_acc = jnp.zeros(own.shape, jnp.float32)
    part_acc = jnp.zeros(partners.shape, jnp.float32)
    for step_no in sorted(range(1, STEPS + 1), key=lambda s: s % groups != 0):
        bands = band_shift(own, groups, step_no)
        field = (bands[:, None] * partners[None]).reshape((-1,) + own.shape[1:])
        field = apply_table("pzyx,xk->pzyk", field, table)
        field = apply_table("pzyx,yk->pzkx", field, table)
        field = lax.all_to_all(field, "slab", split_axis=2, concat_axis=1, tiled=True)
        field = apply_table("pzyx,zk->pkyx", field, table) * kernel
        field = apply_table("pzyx,zk->pkyx", field, table)
        field = lax.all_to_all(field, "slab", split_axis=1, concat_axis=2, tiled=True)
        field = apply_table("pzyx,yk->pzkx", field, table)
        field = apply_table("pzyx,xk->pzyk", field, table)
        potential = field.reshape((own_count, part_count) + own.shape[1:])
        part_acc = part_acc + jnp.sum(potential * bands[:, None], axis=0)
        own_add = jnp.sum(potential * partners[None], axis=1)
        own_acc = own_acc + band_shift(own_add, groups, -step_no)
    return own_acc, part_acc


def two_terms(values):
    high = values.astype(jnp.bfloat16)
    return high, (values - high.astype(jnp.float32)).astype(jnp.bfloat16)


def table_terms(length):
    table = cas_table(length)
    high = table.astype(ml_dtypes.bfloat16)
    low = (table - high.astype(np.float32)).astype(ml_dtypes.bfloat16)
    return high, low


def from_left(high, low, xp=np):
    return xp.concatenate([xp.concatenate([high, high], 1), xp.concatenate([low, low], 1)], 0)


def product(left, right):
    return jnp.dot(left, right, preferred_element_type=jnp.float32)


def along_x(rows, right):
    high, low = two_terms(rows)
    both = product(jnp.concatenate([high, low], 1), right)
    return both[:, : both.shape[1] // 2] + both[:, both.shape[1] // 2 :]


def along_y(columns, left):
    high, low = two_terms(columns)
    both = product(left, jnp.concatenate([high, low], 0))
    return both[: both.shape[0] // 2] + both[both.shape[0] // 2 :]


def steps_of(late):
    steps = []
    for core in range(2):
        for x, z in [(1, 0), (1, 1), (1, 2), (0, 3), (1, 3)] if late else [(0, 0), (0, 1), (0, 2)]:
            steps.append((2 * core + x, z, 4 + 4 * core + z, x))
    return steps


EARLY, LATE = steps_of(False), steps_of(True)


def slabs_of(steps):
    return [(z >> 1) * 8 + (z & 1) * 4 + x * 2 + own // 2 for own, z, part, x in steps]


def used(steps):
    return sorted({step[0] for step in steps} | {step[2] for step in steps})


def to_field(pair_ref, out_ref, right, left):
    rows, length = pair_ref.shape[0], pair_ref.shape[1]
    for r in range(0, rows, 2):
        block = along_x(pair_ref[pl.ds(r, 2)].reshape(2 * length, length), right)
        block = along_y(jnp.concatenate([block[:length], block[length:]], 1), left)
        out_ref[pl.ds(r, length, stride=rows), :] = block[:, :length]
        out_ref[pl.ds(r + 1, length, stride=rows), :] = block[:, length:]


def from_field(field_ref, pot_ref, right, left):
    rows, length = pot_ref.shape[0], pot_ref.shape[1]
    for r in range(0, rows, 2):
        block = jnp.concatenate(
            [field_ref[pl.ds(r + k, length, stride=rows), :] for k in range(2)], 1
        )
        block = along_y(block, left)
        block = jnp.concatenate([block[:, :length], block[:, length:]], 0)
        pot_ref[pl.ds(r, 2)] = along_x(block, right).reshape(2, length, length)


def make_pairs(steps, turn, pieces, pair_ref):
    for k, (own, _, part, _) in enumerate(steps):

        @pl.when(turn == k)
        def _(own=own, part=part):
            pair_ref[...] = pieces[own][0] * pieces[part][0]


def make_terms(steps, turn, pieces, outs, pot_ref):
    for k, (own, _, part, _) in enumerate(steps):

        @pl.when(turn == k)
        def _(own=own, part=part):
            outs[own][0] = pot_ref[...] * pieces[part][0]
            outs[part][0] = pot_ref[...] * pieces[own][0]


def gather_kernel(steps, right_ref, left_ref, *refs):
    pieces, out_ref, pair_ref = dict(zip(used(steps), refs)), refs[-2], refs[-1]
    make_pairs(steps, pl.program_id(0), pieces, pair_ref)
    rows, length = pair_ref.shape[0], pair_ref.shape[1]
    to_field(pair_ref, out_ref.reshape(rows * length, length), right_ref[...], left_ref[...])


def late_kernel(
    steps, groups, right_ref, left_ref, z_left_ref, z_back_ref, square_ref, early_ref, home_ref,
    *refs,
):
    names = used(steps)
    pieces, early_out = dict(zip(names, refs)), refs[len(names)]
    outs = dict(zip(names, refs[len(names) + 1 :]))
    own_ref, part_ref, field_ref, middle_ref, in_sems, out_sems, middle_sems = refs[-7:]
    rows, length = own_ref.shape[1], own_ref.shape[2]
    count, part = len(steps), middle_ref.shape[1]

    def blocks(k, arrays):
        own, z, part, x = steps[k]
        return [(arrays[own].at[z], own_ref.at[k]), (arrays[part].at[x], part_ref.at[k])]

    def fetch(turns, arrays):
        for k in turns:
            for j, (block, held) in enumerate(blocks(k, arrays)):
                pltpu.make_async_copy(block, held, in_sems.at[j, k]).start()

    chosen = [k for k in range(count) if steps[k][0] == 1]
    fetch([k for k in range(count) if k not in chosen], pieces)
    at_home = lax.rem(lax.rem(lax.axis_index("slab"), 2) + 1, groups) == 0

    @pl.when(at_home)
    def _():
        fetch(chosen, {**pieces, 1: home_ref})

    @pl.when(jnp.logical_not(at_home))
    def _():
        fetch(chosen, pieces)

    middle_in = pltpu.make_async_copy(early_ref, middle_ref, middle_sems.at[0])
    middle_in.start()

    @pl.loop(0, count, unroll=5)
    def _(k):
        pltpu.make_async_copy(pieces[names[0]].at[0], own_ref.at[k], in_sems.at[0, k]).wait()
        pltpu.make_async_copy(pieces[names[0]].at[0], part_ref.at[k], in_sems.at[1, k]).wait()
        out_ref = field_ref.at[k]
        for r in range(0, rows, 2):
            pair = own_ref[k, pl.ds(r, 2)] * part_ref[k, pl.ds(r, 2)]
            block = along_x(pair.reshape(2 * length, length), right_ref[...])
            block = along_y(
                jnp.concatenate([block[:length], block[length:]], 1), left_ref[...]
            )
            out_ref[pl.ds(r, length, stride=rows), :] = block[:, :length]
            out_ref[pl.ds(r + 1, length, stride=rows), :] = block[:, length:]

    middle_in.wait()
    group = 32
    scale = coulomb_scale / float(length**3)

    @pl.loop(0, length // group)
    def _(i):
        for k in range(0, group, 2):
            columns, factors, spans = [], [], []
            for j in range(2):
                y = i * group + k + j
                spans.append(pl.ds(pl.multiple_of(y * rows, rows), rows))
                late = field_ref[:, spans[j], :].reshape(count * rows, length)
                columns.append(jnp.concatenate([middle_ref[y], late], 0))
                wave = frequency(y, length)
                total = square_ref[...] + wave * wave
                factors.append(jnp.where(total > 0, scale / jnp.maximum(total, 1.0), 0.0))
            block = along_y(jnp.concatenate(columns, 1), z_left_ref[...])
            block = along_y(block * jnp.concatenate(factors, 1), z_back_ref[...])
            for j in range(2):
                piece = block[:, j * length : (j + 1) * length]
                middle_ref[i * group + k + j] = piece[:part]
                field_ref[:, spans[j], :] = piece[part:].reshape(count, rows, length)

    middle_out = pltpu.make_async_copy(middle_ref, early_out, middle_sems.at[1])
    middle_out.start()

    @pl.loop(0, count, unroll=5)
    def _(k):
        in_ref = field_ref.at[k]
        for r in range(0, rows, 2):
            block = jnp.concatenate(
                [in_ref[pl.ds(r + j, length, stride=rows), :] for j in range(2)], 1
            )
            block = along_y(block, left_ref[...])
            block = jnp.concatenate([block[:, :length], block[:, length:]], 0)
            block = along_x(block, right_ref[...]).reshape(2, length, length)
            span = pl.ds(r, 2)
            own_term = block * part_ref[k, span]
            part_ref[k, span] = block * own_ref[k, span]
            own_ref[k, span] = own_term
        for turn in range(count):

            @pl.when(k == turn)
            def _(turn=turn):
                for j, (block, held) in enumerate(blocks(turn, outs)):
                    pltpu.make_async_copy(held, block, out_sems.at[j, turn]).start()

    for k in range(count):
        for j, (block, held) in enumerate(blocks(k, outs)):
            pltpu.make_async_copy(held, block, out_sems.at[j, k]).wait()
    middle_out.wait()


def scatter_kernel(steps, right_ref, left_ref, field_ref, *refs):
    names = used(steps)
    pieces, outs = dict(zip(names, refs)), dict(zip(names, refs[-1 - len(names) : -1]))
    pot_ref = refs[-1]
    rows, length = pot_ref.shape[0], pot_ref.shape[1]
    flat = field_ref.reshape(rows * length, length)
    from_field(flat, pot_ref, right_ref[...], left_ref[...])
    make_terms(steps, pl.program_id(0), pieces, outs, pot_ref)


def piece_specs(steps, rows, length, starts=(0,)):
    def spec(name):
        visits = []
        for start in starts:
            for turn, (own, z, part, x) in enumerate(steps):
                if name in (own, part):
                    visits.append((start + turn, z if name == own else x))

        def index(i):
            block = visits[0][1]
            for (_, before), (turn, after) in zip(visits, visits[1:]):
                block = block + jnp.where(i >= turn, after - before, 0)
            return (block, 0, 0, 0)

        return pl.BlockSpec((1, rows, length, length), index)

    return [spec(name) for name in used(steps)]


def fixed_spec(shape):
    return pl.BlockSpec(shape, lambda i: (0,) * len(shape))


def settings(megabytes):
    return pltpu.CompilerParams(
        dimension_semantics=("arbitrary",), vmem_limit_bytes=megabytes * 2**20
    )


def cost(cells, length, fields, transforms):
    return pl.CostEstimate(
        flops=transforms * 8 * cells * length, bytes_accessed=4 * fields * cells, transcendentals=0
    )


def gather_part(right, left, pieces, steps):
    rows, length = pieces[0].shape[1], pieces[0].shape[2]
    count = len(steps)
    return pl.pallas_call(
        functools.partial(gather_kernel, steps),
        grid=(count,),
        in_specs=[fixed_spec(right.shape), fixed_spec(left.shape)]
        + piece_specs(steps, rows, length),
        out_specs=pl.BlockSpec((length, rows, length), lambda i: (0, i, 0)),
        out_shape=jax.ShapeDtypeStruct((length, count * rows, length), jnp.float32),
        scratch_shapes=[pltpu.VMEM((rows, length, length), jnp.float32)],
        compiler_params=settings(20),
        cost_estimate=cost(count * rows * length * length, length, 3, 2),
    )(right, left, *[pieces[name] for name in used(steps)])


def late_part(right, left, z_left, z_back, square, early, home, pieces, steps, groups):
    rows, length = pieces[0].shape[1], pieces[0].shape[2]
    names = used(steps)
    count = len(steps)
    tables = [right, left, z_left, z_back, square]
    anywhere = pl.BlockSpec(memory_space=pl.ANY)
    early, *outs = pl.pallas_call(
        functools.partial(late_kernel, steps, groups),
        in_specs=[pl.BlockSpec(memory_space=pltpu.VMEM)] * len(tables)
        + [anywhere] * (2 + len(names)),
        out_specs=[anywhere] * (1 + len(names)),
        out_shape=[jax.ShapeDtypeStruct(early.shape, jnp.float32)]
        + [jax.ShapeDtypeStruct(pieces[name].shape, jnp.float32) for name in names],
        scratch_shapes=[
            pltpu.VMEM((count, rows, length, length), jnp.float32),
            pltpu.VMEM((count, rows, length, length), jnp.float32),
            pltpu.VMEM((count, rows * length, length), jnp.float32),
            pltpu.VMEM(early.shape, jnp.float32),
            pltpu.SemaphoreType.DMA((2, count)),
            pltpu.SemaphoreType.DMA((2, count)),
            pltpu.SemaphoreType.DMA((2,)),
        ],
        compiler_params=pltpu.CompilerParams(vmem_limit_bytes=32 * 2**20),
        cost_estimate=cost(length**3, length, 4, 5),
    )(*tables, early, home, *[pieces[name] for name in names])
    return early, dict(zip(names, outs))


def scatter_part(right, left, field, pieces, steps, held):
    rows, length = pieces[0].shape[1], pieces[0].shape[2]
    names = used(steps)
    specs = piece_specs(steps, rows, length)
    kept = [name for name in names if name in held]
    outs = pl.pallas_call(
        functools.partial(scatter_kernel, steps),
        grid=(len(steps),),
        in_specs=[
            fixed_spec(right.shape), fixed_spec(left.shape),
            pl.BlockSpec((length, rows, length), lambda i: (0, i, 0)),
        ]
        + specs
        + [pl.BlockSpec(memory_space=pl.ANY)] * len(kept),
        out_specs=specs,
        out_shape=[jax.ShapeDtypeStruct(pieces[name].shape, jnp.float32) for name in names],
        input_output_aliases={
            3 + len(names) + k: names.index(name) for k, name in enumerate(kept)
        },
        scratch_shapes=[pltpu.VMEM((rows, length, length), jnp.float32)],
        compiler_params=settings(32),
        cost_estimate=cost(len(steps) * rows * length * length, length, 5, 2),
    )(right, left, field, *[pieces[name] for name in names], *[held[name] for name in kept])
    return dict(zip(names, outs))


def whole_fields(own, partners, groups, slabs):
    length = own.shape[3]
    rows = own.shape[1]
    plane = own.shape[2:]
    me = lax.axis_index("slab")
    part_half, own_band, part_low = (me >> 3) & 1, (me >> 2) & 1, (me >> 1) & 1

    at_home = ((me & 1) + 1) % groups == 0

    def swap(block, mask):
        return lax.ppermute(block, "slab", [(i ^ mask, i) for i in range(slabs)])

    def swap_away(block, mask):
        away = [i for i in range(slabs) if ((i & 1) + 1) % groups != 0]
        return lax.ppermute(block, "slab", [(i ^ mask, i) for i in away])

    def across(block, flip, back):
        route = []
        for b in range(groups):
            for i in range(slabs):
                source = ((b + 1 + (i & 1)) % groups) * slabs + (i ^ flip)
                target = b * slabs + i
                if source != target:
                    route.append((target, source) if back else (source, target))
        return lax.ppermute(block, ("band", "slab"), route)

    def pick(block, position, axis=0):
        return lax.dynamic_index_in_dim(block, position, axis, keepdims=False)

    def ordered(position, mine, other, axis=0):
        shape = [1] * (mine.ndim + 1)
        shape[axis] = 2
        first = lax.iota(jnp.int32, 2).reshape(shape) == position
        return jnp.where(first, jnp.expand_dims(mine, axis), jnp.expand_dims(other, axis))

    def together(*blocks):
        return lax.optimization_barrier(blocks)

    high, low = table_terms(length)
    left = jnp.asarray(from_left(high, low))
    right = jnp.asarray(from_left(high, low).T)
    slab_of = me ^ jnp.asarray(np.array(slabs_of(EARLY) + slabs_of(LATE), np.int32))
    z_high, z_low = [
        jnp.take(jnp.asarray(term).reshape(slabs, rows, length), slab_of, axis=0).reshape(
            length, length
        )
        for term in (high, low)
    ]
    z_left, z_back = from_left(z_high.T, z_low.T, jnp), from_left(z_high, z_low, jnp)
    waves = frequency(lax.iota(jnp.int32, length), length)
    square = waves[:, None] * waves[:, None] + waves[None] * waves[None]

    kept, passed = pick(own, own_band), pick(own, 1 - own_band)
    parts = partners.reshape((2, 2) + partners.shape[1:])
    parts_x = pick(parts, 1 - part_low, 1)
    kept, passed, parts_x = together(kept, passed, parts_x)
    from_z = [swap(kept, 8), swap(passed, 12), swap(passed, 4)]
    parts, parts_x = pick(parts, part_low, 1), swap(parts_x, 2)
    kept_near = jnp.stack([pick(parts, part_half), pick(parts_x, part_half)])
    leaving = jnp.stack([pick(parts, 1 - part_half), pick(parts_x, 1 - part_half)])
    kept_near, leaving, *from_z = together(kept_near, leaving, *from_z)
    got_near, kept_far = swap(leaving, 8), swap(kept_near, 4)
    bands = jnp.stack([kept, from_z[2], from_z[0], from_z[1]])
    bands_x = swap(bands, 2)
    first, second = across(bands, 0, False), across(bands, 1, False)
    bands_x, first, second, got_near, kept_far = together(
        bands_x, first, second, got_near, kept_far
    )
    first_x, second_x = swap_away(first, 2), across(bands_x, 1, False)
    got_far = swap(got_near, 4)
    parts = [kept_near, kept_far, got_near]
    parts_c = [swap(part, 1) for part in parts]
    first = jnp.where(at_home, bands, first)
    early = [first, None, second, None] + parts + [None] + parts_c + [None]
    field_early = gather_part(right, left, early, EARLY)
    got_far, first_x, second_x, field_early = together(got_far, first_x, second_x, field_early)
    pieces = [first, first_x, second, second_x] + parts + [got_far] + parts_c + [swap(got_far, 1)]
    field_early, outs = late_part(
        right, left, z_left, z_back, square, field_early, bands_x, pieces, LATE, groups
    )
    got_far = outs[7] + swap(outs[11], 1)
    got_far, field_early = together(got_far, field_early)
    got_near = swap(got_far, 4)
    first = swap_away(outs[1], 2)
    bands_x = across(outs[3], 1, True) + jnp.where(at_home, outs[1], 0.0)
    outs = scatter_part(right, left, field_early, pieces, EARLY, outs)
    names = sorted(outs)
    first, bands_x, *blocks = together(first, bands_x, *[outs[name] for name in names])
    outs = dict(zip(names, blocks))
    got_near = got_near + outs[6] + swap(outs[10], 1)
    kept_far = outs[5] + swap(outs[9], 1)
    kept_near = outs[4] + swap(outs[8], 1)
    first, second = outs[0] + first, outs[2]
    leaving = swap(got_near, 8)
    kept_near = kept_near + swap(kept_far, 4)
    terms = [across(first, 0, True), across(second, 1, True), swap(bands_x, 2)]
    terms.append(jnp.where(at_home, first, 0.0))
    kept_near, leaving, *terms = together(kept_near, leaving, *terms)
    bands = [sum(term[z] for term in terms) for z in range(4)]
    kept_near, leaving, *bands = together(kept_near, leaving, *bands)
    from_z = [swap(bands[2], 8), swap(bands[3], 12), swap(bands[1], 4)]
    parts_x = swap(ordered(part_half, kept_near[1], leaving[1]), 2)
    parts = ordered(part_low, ordered(part_half, kept_near[0], leaving[0]), parts_x, 1)
    parts, *from_z = together(parts.reshape(partners.shape), *from_z)
    own_out = ordered(own_band, bands[0], from_z[1]) + ordered(own_band, from_z[0], from_z[2])
    return own_out, parts


def solution(mesh):
    groups, slabs = mesh.shape["band"], mesh.shape["slab"]
    spec = P("band", "slab", None, None)

    def shards(own, partners):
        if slabs == 16 and own.shape[0] == 2 and partners.shape[0] == 4 and STEPS == 2:
            return whole_fields(own, partners, groups, slabs)
        return pencils(own, partners, groups, slabs)

    return jax.shard_map(
        shards, mesh=mesh, in_specs=(spec, spec), out_specs=(spec, spec), check_vma=False
    )
```

```python
import functools
import math

import jax
import jax.numpy as jnp
import ml_dtypes
import numpy as np
from jax import lax
from jax.experimental import pallas as pl
from jax.experimental.pallas import tpu as pltpu
from jax.sharding import PartitionSpec as P

STEPS = 2


coulomb_scale = 46.9 * 46.9 / math.pi
precision = lax.Precision.HIGH


def cas_table(length):
    half = length // 2
    angles = np.arange(half) * (2.0 * math.pi / length)
    first = (np.cos(angles) + np.sin(angles)).astype(np.float32)
    wave = np.concatenate([first, -first])
    positions = np.arange(length)
    return wave[(positions[:, None] * positions[None, :]) % length]


def apply_table(pattern, field, table):
    return jnp.einsum(pattern, field, table, precision=precision)


def frequency(positions, length):
    return jnp.where(positions < length // 2, positions, positions - length).astype(jnp.float32)


def coulomb(z_waves, y_waves, x_waves, cells):
    square = (
        z_waves[:, None, None] * z_waves[:, None, None]
        + y_waves[None, :, None] * y_waves[None, :, None]
        + x_waves[None, None, :] * x_waves[None, None, :]
    )
    return jnp.where(square > 0, (coulomb_scale / float(cells)) / jnp.maximum(square, 1.0), 0.0)


def band_shift(block, groups, distance):
    if distance % groups == 0:
        return block
    route = [((b + distance) % groups, b) for b in range(groups)]
    return lax.ppermute(block, "band", route)


def pencils(own, partners, groups, slabs):
    length = own.shape[3]
    own_count, part_count = own.shape[0], partners.shape[0]
    table = jnp.asarray(cas_table(length))
    rows_y = length // slabs
    waves = frequency(lax.iota(jnp.int32, length), length)
    y_waves = frequency(
        lax.axis_index("slab") * rows_y + lax.iota(jnp.int32, rows_y), length
    )
    kernel = coulomb(waves, y_waves, waves, length**3)
    own_acc = jnp.zeros(own.shape, jnp.float32)
    part_acc = jnp.zeros(partners.shape, jnp.float32)
    for step_no in sorted(range(1, STEPS + 1), key=lambda s: s % groups != 0):
        bands = band_shift(own, groups, step_no)
        field = (bands[:, None] * partners[None]).reshape((-1,) + own.shape[1:])
        field = apply_table("pzyx,xk->pzyk", field, table)
        field = apply_table("pzyx,yk->pzkx", field, table)
        field = lax.all_to_all(field, "slab", split_axis=2, concat_axis=1, tiled=True)
        field = apply_table("pzyx,zk->pkyx", field, table) * kernel
        field = apply_table("pzyx,zk->pkyx", field, table)
        field = lax.all_to_all(field, "slab", split_axis=1, concat_axis=2, tiled=True)
        field = apply_table("pzyx,yk->pzkx", field, table)
        field = apply_table("pzyx,xk->pzyk", field, table)
        potential = field.reshape((own_count, part_count) + own.shape[1:])
        part_acc = part_acc + jnp.sum(potential * bands[:, None], axis=0)
        own_add = jnp.sum(potential * partners[None], axis=1)
        own_acc = own_acc + band_shift(own_add, groups, -step_no)
    return own_acc, part_acc


def two_terms(values):
    high = values.astype(jnp.bfloat16)
    return high, (values - high.astype(jnp.float32)).astype(jnp.bfloat16)


def table_terms(length):
    table = cas_table(length)
    high = table.astype(ml_dtypes.bfloat16)
    low = (table - high.astype(np.float32)).astype(ml_dtypes.bfloat16)
    return high, low


def from_left(high, low, xp=np):
    return xp.concatenate([xp.concatenate([high, high], 1), xp.concatenate([low, low], 1)], 0)


def product(left, right):
    return jnp.dot(left, right, preferred_element_type=jnp.float32)


def along_x(rows, right):
    high, low = two_terms(rows)
    both = product(jnp.concatenate([high, low], 1), right)
    return both[:, : both.shape[1] // 2] + both[:, both.shape[1] // 2 :]


def along_y(columns, left):
    high, low = two_terms(columns)
    both = product(left, jnp.concatenate([high, low], 0))
    return both[: both.shape[0] // 2] + both[both.shape[0] // 2 :]


def steps_of(late):
    steps = []
    for core in range(2):
        for x, z in [(1, 0), (1, 1), (1, 2), (0, 3), (1, 3)] if late else [(0, 0), (0, 1), (0, 2)]:
            steps.append((2 * core + x, z, 4 + 4 * core + z, x))
    return steps


EARLY, LATE = steps_of(False), steps_of(True)


def slabs_of(steps):
    return [(z >> 1) * 8 + (z & 1) * 4 + x * 2 + own // 2 for own, z, part, x in steps]


def used(steps):
    return sorted({step[0] for step in steps} | {step[2] for step in steps})


def to_field(pair_ref, out_ref, right, left):
    rows, length = pair_ref.shape[0], pair_ref.shape[1]
    for r in range(0, rows, 2):
        block = along_x(pair_ref[pl.ds(r, 2)].reshape(2 * length, length), right)
        block = along_y(jnp.concatenate([block[:length], block[length:]], 1), left)
        out_ref[pl.ds(r, length, stride=rows), :] = block[:, :length]
        out_ref[pl.ds(r + 1, length, stride=rows), :] = block[:, length:]


def from_field(field_ref, pot_ref, right, left):
    rows, length = pot_ref.shape[0], pot_ref.shape[1]
    for r in range(0, rows, 2):
        block = jnp.concatenate(
            [field_ref[pl.ds(r + k, length, stride=rows), :] for k in range(2)], 1
        )
        block = along_y(block, left)
        block = jnp.concatenate([block[:, :length], block[:, length:]], 0)
        pot_ref[pl.ds(r, 2)] = along_x(block, right).reshape(2, length, length)


def make_pairs(steps, turn, pieces, pair_ref):
    for k, (own, _, part, _) in enumerate(steps):

        @pl.when(turn == k)
        def _(own=own, part=part):
            pair_ref[...] = pieces[own][0] * pieces[part][0]


def make_terms(steps, turn, pieces, outs, pot_ref):
    for k, (own, _, part, _) in enumerate(steps):

        @pl.when(turn == k)
        def _(own=own, part=part):
            outs[own][0] = pot_ref[...] * pieces[part][0]
            outs[part][0] = pot_ref[...] * pieces[own][0]


def gather_kernel(steps, right_ref, left_ref, *refs):
    pieces, out_ref, pair_ref = dict(zip(used(steps), refs)), refs[-2], refs[-1]
    make_pairs(steps, pl.program_id(0), pieces, pair_ref)
    rows, length = pair_ref.shape[0], pair_ref.shape[1]
    to_field(pair_ref, out_ref.reshape(rows * length, length), right_ref[...], left_ref[...])


def late_kernel(
    steps, groups, right_ref, left_ref, z_left_ref, z_back_ref, square_ref, early_ref, home_ref,
    *refs,
):
    names = used(steps)
    pieces, early_out = dict(zip(names, refs)), refs[len(names)]
    outs = dict(zip(names, refs[len(names) + 1 :]))
    own_ref, part_ref, field_ref, middle_ref, in_sems, out_sems, middle_sems = refs[-7:]
    rows, length = own_ref.shape[1], own_ref.shape[2]
    count, part = len(steps), middle_ref.shape[1]

    def blocks(k, arrays):
        own, z, part, x = steps[k]
        return [(arrays[own].at[z], own_ref.at[k]), (arrays[part].at[x], part_ref.at[k])]

    def fetch(turns, arrays):
        for k in turns:
            for j, (block, held) in enumerate(blocks(k, arrays)):
                pltpu.make_async_copy(block, held, in_sems.at[j, k]).start()

    chosen = [k for k in range(count) if steps[k][0] == 1]
    at_home = lax.rem(lax.rem(lax.axis_index("slab"), 2) + 1, groups) == 0

    @pl.when(at_home)
    def _():
        fetch(chosen, {**pieces, 1: home_ref})

    @pl.when(jnp.logical_not(at_home))
    def _():
        fetch(chosen, pieces)

    fetch([k for k in range(count) if k not in chosen], pieces)
    middle_in = pltpu.make_async_copy(early_ref, middle_ref, middle_sems.at[0])
    middle_in.start()

    @pl.loop(0, count, unroll=5)
    def _(k):
        pltpu.make_async_copy(pieces[names[0]].at[0], own_ref.at[k], in_sems.at[0, k]).wait()
        pltpu.make_async_copy(pieces[names[0]].at[0], part_ref.at[k], in_sems.at[1, k]).wait()
        out_ref = field_ref.at[k]
        for r in range(0, rows, 2):
            pair = own_ref[k, pl.ds(r, 2)] * part_ref[k, pl.ds(r, 2)]
            block = along_x(pair.reshape(2 * length, length), right_ref[...])
            block = along_y(
                jnp.concatenate([block[:length], block[length:]], 1), left_ref[...]
            )
            out_ref[pl.ds(r, length, stride=rows), :] = block[:, :length]
            out_ref[pl.ds(r + 1, length, stride=rows), :] = block[:, length:]

    middle_in.wait()
    group = 32
    scale = coulomb_scale / float(length**3)

    @pl.loop(0, length // group)
    def _(i):
        for k in range(0, group, 2):
            columns, factors, spans = [], [], []
            for j in range(2):
                y = i * group + k + j
                spans.append(pl.ds(pl.multiple_of(y * rows, rows), rows))
                late = field_ref[:, spans[j], :].reshape(count * rows, length)
                columns.append(jnp.concatenate([middle_ref[y], late], 0))
                wave = frequency(y, length)
                total = square_ref[...] + wave * wave
                factors.append(jnp.where(total > 0, scale / jnp.maximum(total, 1.0), 0.0))
            block = along_y(jnp.concatenate(columns, 1), z_left_ref[...])
            block = along_y(block * jnp.concatenate(factors, 1), z_back_ref[...])
            for j in range(2):
                piece = block[:, j * length : (j + 1) * length]
                middle_ref[i * group + k + j] = piece[:part]
                field_ref[:, spans[j], :] = piece[part:].reshape(count, rows, length)

    middle_out = pltpu.make_async_copy(middle_ref, early_out, middle_sems.at[1])
    middle_out.start()

    @pl.loop(0, count, unroll=5)
    def _(k):
        in_ref = field_ref.at[k]
        for r in range(0, rows, 2):
            block = jnp.concatenate(
                [in_ref[pl.ds(r + j, length, stride=rows), :] for j in range(2)], 1
            )
            block = along_y(block, left_ref[...])
            block = jnp.concatenate([block[:, :length], block[:, length:]], 0)
            block = along_x(block, right_ref[...]).reshape(2, length, length)
            span = pl.ds(r, 2)
            own_term = block * part_ref[k, span]
            part_ref[k, span] = block * own_ref[k, span]
            own_ref[k, span] = own_term
        for turn in range(count):

            @pl.when(k == turn)
            def _(turn=turn):
                for j, (block, held) in enumerate(blocks(turn, outs)):
                    pltpu.make_async_copy(held, block, out_sems.at[j, turn]).start()

    for k in range(count):
        for j, (block, held) in enumerate(blocks(k, outs)):
            pltpu.make_async_copy(held, block, out_sems.at[j, k]).wait()
    middle_out.wait()


def scatter_kernel(steps, right_ref, left_ref, field_ref, *refs):
    names = used(steps)
    pieces, outs = dict(zip(names, refs)), dict(zip(names, refs[-1 - len(names) : -1]))
    pot_ref = refs[-1]
    rows, length = pot_ref.shape[0], pot_ref.shape[1]
    flat = field_ref.reshape(rows * length, length)
    from_field(flat, pot_ref, right_ref[...], left_ref[...])
    make_terms(steps, pl.program_id(0), pieces, outs, pot_ref)


def piece_specs(steps, rows, length, starts=(0,)):
    def spec(name):
        visits = []
        for start in starts:
            for turn, (own, z, part, x) in enumerate(steps):
                if name in (own, part):
                    visits.append((start + turn, z if name == own else x))

        def index(i):
            block = visits[0][1]
            for (_, before), (turn, after) in zip(visits, visits[1:]):
                block = block + jnp.where(i >= turn, after - before, 0)
            return (block, 0, 0, 0)

        return pl.BlockSpec((1, rows, length, length), index)

    return [spec(name) for name in used(steps)]


def fixed_spec(shape):
    return pl.BlockSpec(shape, lambda i: (0,) * len(shape))


def settings(megabytes):
    return pltpu.CompilerParams(
        dimension_semantics=("arbitrary",), vmem_limit_bytes=megabytes * 2**20
    )


def cost(cells, length, fields, transforms):
    return pl.CostEstimate(
        flops=transforms * 8 * cells * length, bytes_accessed=4 * fields * cells, transcendentals=0
    )


def gather_part(right, left, pieces, steps):
    rows, length = pieces[0].shape[1], pieces[0].shape[2]
    count = len(steps)
    return pl.pallas_call(
        functools.partial(gather_kernel, steps),
        grid=(count,),
        in_specs=[fixed_spec(right.shape), fixed_spec(left.shape)]
        + piece_specs(steps, rows, length),
        out_specs=pl.BlockSpec((length, rows, length), lambda i: (0, i, 0)),
        out_shape=jax.ShapeDtypeStruct((length, count * rows, length), jnp.float32),
        scratch_shapes=[pltpu.VMEM((rows, length, length), jnp.float32)],
        compiler_params=settings(20),
        cost_estimate=cost(count * rows * length * length, length, 3, 2),
    )(right, left, *[pieces[name] for name in used(steps)])


def late_part(right, left, z_left, z_back, square, early, home, pieces, steps, groups):
    rows, length = pieces[0].shape[1], pieces[0].shape[2]
    names = used(steps)
    count = len(steps)
    tables = [right, left, z_left, z_back, square]
    anywhere = pl.BlockSpec(memory_space=pl.ANY)
    early, *outs = pl.pallas_call(
        functools.partial(late_kernel, steps, groups),
        in_specs=[pl.BlockSpec(memory_space=pltpu.VMEM)] * len(tables)
        + [anywhere] * (2 + len(names)),
        out_specs=[anywhere] * (1 + len(names)),
        out_shape=[jax.ShapeDtypeStruct(early.shape, jnp.float32)]
        + [jax.ShapeDtypeStruct(pieces[name].shape, jnp.float32) for name in names],
        scratch_shapes=[
            pltpu.VMEM((count, rows, length, length), jnp.float32),
            pltpu.VMEM((count, rows, length, length), jnp.float32),
            pltpu.VMEM((count, rows * length, length), jnp.float32),
            pltpu.VMEM(early.shape, jnp.float32),
            pltpu.SemaphoreType.DMA((2, count)),
            pltpu.SemaphoreType.DMA((2, count)),
            pltpu.SemaphoreType.DMA((2,)),
        ],
        compiler_params=pltpu.CompilerParams(vmem_limit_bytes=32 * 2**20),
        cost_estimate=cost(length**3, length, 4, 5),
    )(*tables, early, home, *[pieces[name] for name in names])
    return early, dict(zip(names, outs))


def scatter_part(right, left, field, pieces, steps, held):
    rows, length = pieces[0].shape[1], pieces[0].shape[2]
    names = used(steps)
    specs = piece_specs(steps, rows, length)
    kept = [name for name in names if name in held]
    outs = pl.pallas_call(
        functools.partial(scatter_kernel, steps),
        grid=(len(steps),),
        in_specs=[
            fixed_spec(right.shape), fixed_spec(left.shape),
            pl.BlockSpec((length, rows, length), lambda i: (0, i, 0)),
        ]
        + specs
        + [pl.BlockSpec(memory_space=pl.ANY)] * len(kept),
        out_specs=specs,
        out_shape=[jax.ShapeDtypeStruct(pieces[name].shape, jnp.float32) for name in names],
        input_output_aliases={
            3 + len(names) + k: names.index(name) for k, name in enumerate(kept)
        },
        scratch_shapes=[pltpu.VMEM((rows, length, length), jnp.float32)],
        compiler_params=settings(32),
        cost_estimate=cost(len(steps) * rows * length * length, length, 5, 2),
    )(right, left, field, *[pieces[name] for name in names], *[held[name] for name in kept])
    return dict(zip(names, outs))


def whole_fields(own, partners, groups, slabs):
    length = own.shape[3]
    rows = own.shape[1]
    plane = own.shape[2:]
    me = lax.axis_index("slab")
    part_half, own_band, part_low = (me >> 3) & 1, (me >> 2) & 1, (me >> 1) & 1

    at_home = ((me & 1) + 1) % groups == 0

    def swap(block, mask):
        return lax.ppermute(block, "slab", [(i ^ mask, i) for i in range(slabs)])

    def swap_away(block, mask):
        away = [i for i in range(slabs) if ((i & 1) + 1) % groups != 0]
        return lax.ppermute(block, "slab", [(i ^ mask, i) for i in away])

    def across(block, flip, back):
        route = []
        for b in range(groups):
            for i in range(slabs):
                source = ((b + 1 + (i & 1)) % groups) * slabs + (i ^ flip)
                target = b * slabs + i
                if source != target:
                    route.append((target, source) if back else (source, target))
        return lax.ppermute(block, ("band", "slab"), route)

    def pick(block, position, axis=0):
        return lax.dynamic_index_in_dim(block, position, axis, keepdims=False)

    def ordered(position, mine, other, axis=0):
        shape = [1] * (mine.ndim + 1)
        shape[axis] = 2
        first = lax.iota(jnp.int32, 2).reshape(shape) == position
        return jnp.where(first, jnp.expand_dims(mine, axis), jnp.expand_dims(other, axis))

    def together(*blocks):
        return lax.optimization_barrier(blocks)

    high, low = table_terms(length)
    left = jnp.asarray(from_left(high, low))
    right = jnp.asarray(from_left(high, low).T)
    slab_of = me ^ jnp.asarray(np.array(slabs_of(EARLY) + slabs_of(LATE), np.int32))
    z_high, z_low = [
        jnp.take(jnp.asarray(term).reshape(slabs, rows, length), slab_of, axis=0).reshape(
            length, length
        )
        for term in (high, low)
    ]
    z_left, z_back = from_left(z_high.T, z_low.T, jnp), from_left(z_high, z_low, jnp)
    waves = frequency(lax.iota(jnp.int32, length), length)
    square = waves[:, None] * waves[:, None] + waves[None] * waves[None]

    kept, passed = pick(own, own_band), pick(own, 1 - own_band)
    parts = partners.reshape((2, 2) + partners.shape[1:])
    parts_x = pick(parts, 1 - part_low, 1)
    kept, passed, parts_x = together(kept, passed, parts_x)
    from_z = [swap(kept, 8), swap(passed, 12), swap(passed, 4)]
    parts, parts_x = pick(parts, part_low, 1), swap(parts_x, 2)
    kept_near = jnp.stack([pick(parts, part_half), pick(parts_x, part_half)])
    leaving = jnp.stack([pick(parts, 1 - part_half), pick(parts_x, 1 - part_half)])
    kept_near, leaving, *from_z = together(kept_near, leaving, *from_z)
    got_near, kept_far = swap(leaving, 8), swap(kept_near, 4)
    bands = jnp.stack([kept, from_z[2], from_z[0], from_z[1]])
    bands_x = swap(bands, 2)
    first, second = across(bands, 0, False), across(bands, 1, False)
    bands_x, first, second, got_near, kept_far = together(
        bands_x, first, second, got_near, kept_far
    )
    first_x, second_x = swap_away(first, 2), across(bands_x, 1, False)
    got_far = swap(got_near, 4)
    parts = [kept_near, kept_far, got_near]
    parts_c = [swap(part, 1) for part in parts]
    first = jnp.where(at_home, bands, first)
    early = [first, None, second, None] + parts + [None] + parts_c + [None]
    field_early = gather_part(right, left, early, EARLY)
    got_far, first_x, second_x, field_early = together(got_far, first_x, second_x, field_early)
    pieces = [first, first_x, second, second_x] + parts + [got_far] + parts_c + [swap(got_far, 1)]
    field_early, outs = late_part(
        right, left, z_left, z_back, square, field_early, bands_x, pieces, LATE, groups
    )
    got_far = outs[7] + swap(outs[11], 1)
    got_far, field_early = together(got_far, field_early)
    got_near = swap(got_far, 4)
    first = swap_away(outs[1], 2)
    bands_x = across(outs[3], 1, True) + jnp.where(at_home, outs[1], 0.0)
    outs = scatter_part(right, left, field_early, pieces, EARLY, outs)
    names = sorted(outs)
    first, bands_x, *blocks = together(first, bands_x, *[outs[name] for name in names])
    outs = dict(zip(names, blocks))
    got_near = got_near + outs[6] + swap(outs[10], 1)
    kept_far = outs[5] + swap(outs[9], 1)
    kept_near = outs[4] + swap(outs[8], 1)
    first, second = outs[0] + first, outs[2]
    leaving = swap(got_near, 8)
    kept_near = kept_near + swap(kept_far, 4)
    terms = [across(first, 0, True), across(second, 1, True), swap(bands_x, 2)]
    terms.append(jnp.where(at_home, first, 0.0))
    kept_near, leaving, *terms = together(kept_near, leaving, *terms)
    bands = [sum(term[z] for term in terms) for z in range(4)]
    kept_near, leaving, *bands = together(kept_near, leaving, *bands)
    from_z = [swap(bands[2], 8), swap(bands[3], 12), swap(bands[1], 4)]
    parts_x = swap(ordered(part_half, kept_near[1], leaving[1]), 2)
    parts = ordered(part_low, ordered(part_half, kept_near[0], leaving[0]), parts_x, 1)
    parts, *from_z = together(parts.reshape(partners.shape), *from_z)
    own_out = ordered(own_band, bands[0], from_z[1]) + ordered(own_band, from_z[0], from_z[2])
    return own_out, parts


def solution(mesh):
    groups, slabs = mesh.shape["band"], mesh.shape["slab"]
    spec = P("band", "slab", None, None)

    def shards(own, partners):
        if slabs == 16 and own.shape[0] == 2 and partners.shape[0] == 4 and STEPS == 2:
            return whole_fields(own, partners, groups, slabs)
        return pencils(own, partners, groups, slabs)

    return jax.shard_map(
        shards, mesh=mesh, in_specs=(spec, spec), out_specs=(spec, spec), check_vma=False
    )
```

```python
import functools
import math

import jax
import jax.numpy as jnp
import ml_dtypes
import numpy as np
from jax import lax
from jax.experimental import pallas as pl
from jax.experimental.pallas import tpu as pltpu
from jax.sharding import PartitionSpec as P

STEPS = 2


coulomb_scale = 46.9 * 46.9 / math.pi
precision = lax.Precision.HIGH


def cas_table(length):
    half = length // 2
    angles = np.arange(half) * (2.0 * math.pi / length)
    first = (np.cos(angles) + np.sin(angles)).astype(np.float32)
    wave = np.concatenate([first, -first])
    positions = np.arange(length)
    return wave[(positions[:, None] * positions[None, :]) % length]


def apply_table(pattern, field, table):
    return jnp.einsum(pattern, field, table, precision=precision)


def frequency(positions, length):
    return jnp.where(positions < length // 2, positions, positions - length).astype(jnp.float32)


def coulomb(z_waves, y_waves, x_waves, cells):
    square = (
        z_waves[:, None, None] * z_waves[:, None, None]
        + y_waves[None, :, None] * y_waves[None, :, None]
        + x_waves[None, None, :] * x_waves[None, None, :]
    )
    return jnp.where(square > 0, (coulomb_scale / float(cells)) / jnp.maximum(square, 1.0), 0.0)


def band_shift(block, groups, distance):
    if distance % groups == 0:
        return block
    route = [((b + distance) % groups, b) for b in range(groups)]
    return lax.ppermute(block, "band", route)


def pencils(own, partners, groups, slabs):
    length = own.shape[3]
    own_count, part_count = own.shape[0], partners.shape[0]
    table = jnp.asarray(cas_table(length))
    rows_y = length // slabs
    waves = frequency(lax.iota(jnp.int32, length), length)
    y_waves = frequency(
        lax.axis_index("slab") * rows_y + lax.iota(jnp.int32, rows_y), length
    )
    kernel = coulomb(waves, y_waves, waves, length**3)
    own_acc = jnp.zeros(own.shape, jnp.float32)
    part_acc = jnp.zeros(partners.shape, jnp.float32)
    for step_no in sorted(range(1, STEPS + 1), key=lambda s: s % groups != 0):
        bands = band_shift(own, groups, step_no)
        field = (bands[:, None] * partners[None]).reshape((-1,) + own.shape[1:])
        field = apply_table("pzyx,xk->pzyk", field, table)
        field = apply_table("pzyx,yk->pzkx", field, table)
        field = lax.all_to_all(field, "slab", split_axis=2, concat_axis=1, tiled=True)
        field = apply_table("pzyx,zk->pkyx", field, table) * kernel
        field = apply_table("pzyx,zk->pkyx", field, table)
        field = lax.all_to_all(field, "slab", split_axis=1, concat_axis=2, tiled=True)
        field = apply_table("pzyx,yk->pzkx", field, table)
        field = apply_table("pzyx,xk->pzyk", field, table)
        potential = field.reshape((own_count, part_count) + own.shape[1:])
        part_acc = part_acc + jnp.sum(potential * bands[:, None], axis=0)
        own_add = jnp.sum(potential * partners[None], axis=1)
        own_acc = own_acc + band_shift(own_add, groups, -step_no)
    return own_acc, part_acc


def two_terms(values):
    high = values.astype(jnp.bfloat16)
    return high, (values - high.astype(jnp.float32)).astype(jnp.bfloat16)


def table_terms(length):
    table = cas_table(length)
    high = table.astype(ml_dtypes.bfloat16)
    low = (table - high.astype(np.float32)).astype(ml_dtypes.bfloat16)
    return high, low


def from_left(high, low, xp=np):
    return xp.concatenate([xp.concatenate([high, high], 1), xp.concatenate([low, low], 1)], 0)


def product(left, right):
    return jnp.dot(left, right, preferred_element_type=jnp.float32)


def along_x(rows, right):
    high, low = two_terms(rows)
    both = product(jnp.concatenate([high, low], 1), right)
    return both[:, : both.shape[1] // 2] + both[:, both.shape[1] // 2 :]


def along_y(columns, left):
    high, low = two_terms(columns)
    both = product(left, jnp.concatenate([high, low], 0))
    return both[: both.shape[0] // 2] + both[both.shape[0] // 2 :]


def steps_of(late):
    steps = []
    for core in range(2):
        for x, z in [(1, 0), (1, 1), (1, 2), (0, 3), (1, 3)] if late else [(0, 0), (0, 1), (0, 2)]:
            steps.append((2 * core + x, z, 4 + 4 * core + z, x))
    return steps


EARLY, LATE = steps_of(False), steps_of(True)


def slabs_of(steps):
    return [(z >> 1) * 8 + (z & 1) * 4 + x * 2 + own // 2 for own, z, part, x in steps]


def used(steps):
    return sorted({step[0] for step in steps} | {step[2] for step in steps})


def to_field(pair_ref, out_ref, right, left):
    rows, length = pair_ref.shape[0], pair_ref.shape[1]
    for r in range(0, rows, 2):
        block = along_x(pair_ref[pl.ds(r, 2)].reshape(2 * length, length), right)
        block = along_y(jnp.concatenate([block[:length], block[length:]], 1), left)
        out_ref[pl.ds(r, length, stride=rows), :] = block[:, :length]
        out_ref[pl.ds(r + 1, length, stride=rows), :] = block[:, length:]


def from_field(field_ref, pot_ref, right, left):
    rows, length = pot_ref.shape[0], pot_ref.shape[1]
    for r in range(0, rows, 2):
        block = jnp.concatenate(
            [field_ref[pl.ds(r + k, length, stride=rows), :] for k in range(2)], 1
        )
        block = along_y(block, left)
        block = jnp.concatenate([block[:, :length], block[:, length:]], 0)
        pot_ref[pl.ds(r, 2)] = along_x(block, right).reshape(2, length, length)


def make_pairs(steps, turn, pieces, pair_ref):
    for k, (own, _, part, _) in enumerate(steps):

        @pl.when(turn == k)
        def _(own=own, part=part):
            pair_ref[...] = pieces[own][0] * pieces[part][0]


def make_terms(steps, turn, pieces, outs, pot_ref):
    for k, (own, _, part, _) in enumerate(steps):

        @pl.when(turn == k)
        def _(own=own, part=part):
            outs[own][0] = pot_ref[...] * pieces[part][0]
            outs[part][0] = pot_ref[...] * pieces[own][0]


def gather_kernel(steps, right_ref, left_ref, *refs):
    pieces, out_ref, pair_ref = dict(zip(used(steps), refs)), refs[-2], refs[-1]
    make_pairs(steps, pl.program_id(0), pieces, pair_ref)
    rows, length = pair_ref.shape[0], pair_ref.shape[1]
    to_field(pair_ref, out_ref.reshape(rows * length, length), right_ref[...], left_ref[...])


def late_kernel(
    steps, groups, right_ref, left_ref, z_left_ref, z_back_ref, square_ref, early_ref, home_ref,
    *refs,
):
    names = used(steps)
    pieces, early_out = dict(zip(names, refs)), refs[len(names)]
    outs = dict(zip(names, refs[len(names) + 1 :]))
    own_ref, part_ref, field_ref, middle_ref, in_sems, out_sems, middle_sems = refs[-7:]
    rows, length = own_ref.shape[1], own_ref.shape[2]
    count, part = len(steps), middle_ref.shape[1]

    def blocks(k, arrays):
        own, z, part, x = steps[k]
        return [(arrays[own].at[z], own_ref.at[k]), (arrays[part].at[x], part_ref.at[k])]

    def fetch(turns, arrays):
        for k in turns:
            for j, (block, held) in enumerate(blocks(k, arrays)):
                pltpu.make_async_copy(block, held, in_sems.at[j, k]).start()

    chosen = [k for k in range(count) if steps[k][0] == 1]
    at_home = lax.rem(lax.rem(lax.axis_index("slab"), 2) + 1, groups) == 0

    @pl.when(at_home)
    def _():
        fetch(chosen, {**pieces, 1: home_ref})

    @pl.when(jnp.logical_not(at_home))
    def _():
        fetch(chosen, pieces)

    fetch([k for k in range(count) if k not in chosen], pieces)
    middle_in = pltpu.make_async_copy(early_ref, middle_ref, middle_sems.at[0])
    middle_in.start()

    @pl.loop(0, count, unroll=5)
    def _(k):
        pltpu.make_async_copy(pieces[names[0]].at[0], own_ref.at[k], in_sems.at[0, k]).wait()
        pltpu.make_async_copy(pieces[names[0]].at[0], part_ref.at[k], in_sems.at[1, k]).wait()
        out_ref = field_ref.at[k]
        for r in range(0, rows, 2):
            pair = own_ref[k, pl.ds(r, 2)] * part_ref[k, pl.ds(r, 2)]
            block = along_x(pair.reshape(2 * length, length), right_ref[...])
            block = along_y(
                jnp.concatenate([block[:length], block[length:]], 1), left_ref[...]
            )
            out_ref[pl.ds(r, length, stride=rows), :] = block[:, :length]
            out_ref[pl.ds(r + 1, length, stride=rows), :] = block[:, length:]

    middle_in.wait()
    group = 32
    scale = coulomb_scale / float(length**3)

    @pl.loop(0, length // group)
    def _(i):
        for k in range(0, group, 2):
            columns, factors, spans = [], [], []
            for j in range(2):
                y = i * group + k + j
                spans.append(pl.ds(pl.multiple_of(y * rows, rows), rows))
                late = field_ref[:, spans[j], :].reshape(count * rows, length)
                columns.append(jnp.concatenate([middle_ref[y], late], 0))
                wave = frequency(y, length)
                total = square_ref[...] + wave * wave
                factors.append(jnp.where(total > 0, scale / jnp.maximum(total, 1.0), 0.0))
            block = along_y(jnp.concatenate(columns, 1), z_left_ref[...])
            block = along_y(block * jnp.concatenate(factors, 1), z_back_ref[...])
            for j in range(2):
                piece = block[:, j * length : (j + 1) * length]
                middle_ref[i * group + k + j] = piece[:part]
                field_ref[:, spans[j], :] = piece[part:].reshape(count, rows, length)

    middle_out = pltpu.make_async_copy(middle_ref, early_out, middle_sems.at[1])
    middle_out.start()

    @pl.loop(0, count, unroll=5)
    def _(k):
        in_ref = field_ref.at[k]
        for r in range(0, rows, 2):
            block = jnp.concatenate(
                [in_ref[pl.ds(r + j, length, stride=rows), :] for j in range(2)], 1
            )
            block = along_y(block, left_ref[...])
            block = jnp.concatenate([block[:, :length], block[:, length:]], 0)
            block = along_x(block, right_ref[...]).reshape(2, length, length)
            span = pl.ds(r, 2)
            own_term = block * part_ref[k, span]
            part_ref[k, span] = block * own_ref[k, span]
            own_ref[k, span] = own_term
        for turn in range(count):

            @pl.when(k == turn)
            def _(turn=turn):
                for j, (block, held) in enumerate(blocks(turn, outs)):
                    pltpu.make_async_copy(held, block, out_sems.at[j, turn]).start()

    for k in range(count):
        for j, (block, held) in enumerate(blocks(k, outs)):
            pltpu.make_async_copy(held, block, out_sems.at[j, k]).wait()
    middle_out.wait()


def scatter_kernel(steps, right_ref, left_ref, field_ref, *refs):
    names = used(steps)
    pieces, outs = dict(zip(names, refs)), dict(zip(names, refs[-1 - len(names) : -1]))
    pot_ref = refs[-1]
    rows, length = pot_ref.shape[0], pot_ref.shape[1]
    flat = field_ref.reshape(rows * length, length)
    from_field(flat, pot_ref, right_ref[...], left_ref[...])
    make_terms(steps, pl.program_id(0), pieces, outs, pot_ref)


def piece_specs(steps, rows, length, starts=(0,)):
    def spec(name):
        visits = []
        for start in starts:
            for turn, (own, z, part, x) in enumerate(steps):
                if name in (own, part):
                    visits.append((start + turn, z if name == own else x))

        def index(i):
            block = visits[0][1]
            for (_, before), (turn, after) in zip(visits, visits[1:]):
                block = block + jnp.where(i >= turn, after - before, 0)
            return (block, 0, 0, 0)

        return pl.BlockSpec((1, rows, length, length), index)

    return [spec(name) for name in used(steps)]


def fixed_spec(shape):
    return pl.BlockSpec(shape, lambda i: (0,) * len(shape))


def settings(megabytes):
    return pltpu.CompilerParams(
        dimension_semantics=("arbitrary",), vmem_limit_bytes=megabytes * 2**20
    )


def cost(cells, length, fields, transforms):
    return pl.CostEstimate(
        flops=transforms * 8 * cells * length, bytes_accessed=4 * fields * cells, transcendentals=0
    )


def gather_part(right, left, pieces, steps):
    rows, length = pieces[0].shape[1], pieces[0].shape[2]
    count = len(steps)
    return pl.pallas_call(
        functools.partial(gather_kernel, steps),
        grid=(count,),
        in_specs=[fixed_spec(right.shape), fixed_spec(left.shape)]
        + piece_specs(steps, rows, length),
        out_specs=pl.BlockSpec((length, rows, length), lambda i: (0, i, 0)),
        out_shape=jax.ShapeDtypeStruct((length, count * rows, length), jnp.float32),
        scratch_shapes=[pltpu.VMEM((rows, length, length), jnp.float32)],
        compiler_params=settings(20),
        cost_estimate=cost(count * rows * length * length, length, 3, 2),
    )(right, left, *[pieces[name] for name in used(steps)])


def late_part(right, left, z_left, z_back, square, early, home, pieces, steps, groups):
    rows, length = pieces[0].shape[1], pieces[0].shape[2]
    names = used(steps)
    count = len(steps)
    tables = [right, left, z_left, z_back, square]
    anywhere = pl.BlockSpec(memory_space=pl.ANY)
    early, *outs = pl.pallas_call(
        functools.partial(late_kernel, steps, groups),
        in_specs=[pl.BlockSpec(memory_space=pltpu.VMEM)] * len(tables)
        + [anywhere] * (2 + len(names)),
        out_specs=[anywhere] * (1 + len(names)),
        out_shape=[jax.ShapeDtypeStruct(early.shape, jnp.float32)]
        + [jax.ShapeDtypeStruct(pieces[name].shape, jnp.float32) for name in names],
        scratch_shapes=[
            pltpu.VMEM((count, rows, length, length), jnp.float32),
            pltpu.VMEM((count, rows, length, length), jnp.float32),
            pltpu.VMEM((count, rows * length, length), jnp.float32),
            pltpu.VMEM(early.shape, jnp.float32),
            pltpu.SemaphoreType.DMA((2, count)),
            pltpu.SemaphoreType.DMA((2, count)),
            pltpu.SemaphoreType.DMA((2,)),
        ],
        compiler_params=pltpu.CompilerParams(vmem_limit_bytes=32 * 2**20),
        cost_estimate=cost(length**3, length, 4, 5),
    )(*tables, early, home, *[pieces[name] for name in names])
    return early, dict(zip(names, outs))


def scatter_part(right, left, field, pieces, steps, held):
    rows, length = pieces[0].shape[1], pieces[0].shape[2]
    names = used(steps)
    specs = piece_specs(steps, rows, length)
    kept = [name for name in names if name in held]
    outs = pl.pallas_call(
        functools.partial(scatter_kernel, steps),
        grid=(len(steps),),
        in_specs=[
            fixed_spec(right.shape), fixed_spec(left.shape),
            pl.BlockSpec((length, rows, length), lambda i: (0, i, 0)),
        ]
        + specs
        + [pl.BlockSpec(memory_space=pl.ANY)] * len(kept),
        out_specs=specs,
        out_shape=[jax.ShapeDtypeStruct(pieces[name].shape, jnp.float32) for name in names],
        input_output_aliases={
            3 + len(names) + k: names.index(name) for k, name in enumerate(kept)
        },
        scratch_shapes=[pltpu.VMEM((rows, length, length), jnp.float32)],
        compiler_params=settings(32),
        cost_estimate=cost(len(steps) * rows * length * length, length, 5, 2),
    )(right, left, field, *[pieces[name] for name in names], *[held[name] for name in kept])
    return dict(zip(names, outs))


def whole_fields(own, partners, groups, slabs):
    length = own.shape[3]
    rows = own.shape[1]
    plane = own.shape[2:]
    me = lax.axis_index("slab")
    part_half, own_band, part_low = (me >> 3) & 1, (me >> 2) & 1, (me >> 1) & 1

    at_home = ((me & 1) + 1) % groups == 0

    def swap(block, mask):
        return lax.ppermute(block, "slab", [(i ^ mask, i) for i in range(slabs)])

    def swap_away(block, mask):
        away = [i for i in range(slabs) if ((i & 1) + 1) % groups != 0]
        return lax.ppermute(block, "slab", [(i ^ mask, i) for i in away])

    def across(block, flip, back):
        route = []
        for b in range(groups):
            for i in range(slabs):
                source = ((b + 1 + (i & 1)) % groups) * slabs + (i ^ flip)
                target = b * slabs + i
                if source != target:
                    route.append((target, source) if back else (source, target))
        return lax.ppermute(block, ("band", "slab"), route)

    def pick(block, position, axis=0):
        return lax.dynamic_index_in_dim(block, position, axis, keepdims=False)

    def ordered(position, mine, other, axis=0):
        shape = [1] * (mine.ndim + 1)
        shape[axis] = 2
        first = lax.iota(jnp.int32, 2).reshape(shape) == position
        return jnp.where(first, jnp.expand_dims(mine, axis), jnp.expand_dims(other, axis))

    def together(*blocks):
        return lax.optimization_barrier(blocks)

    high, low = table_terms(length)
    left = jnp.asarray(from_left(high, low))
    right = jnp.asarray(from_left(high, low).T)
    slab_of = me ^ jnp.asarray(np.array(slabs_of(EARLY) + slabs_of(LATE), np.int32))
    z_high, z_low = [
        jnp.take(jnp.asarray(term).reshape(slabs, rows, length), slab_of, axis=0).reshape(
            length, length
        )
        for term in (high, low)
    ]
    z_left, z_back = from_left(z_high.T, z_low.T, jnp), from_left(z_high, z_low, jnp)
    waves = frequency(lax.iota(jnp.int32, length), length)
    square = waves[:, None] * waves[:, None] + waves[None] * waves[None]

    kept, passed = pick(own, own_band), pick(own, 1 - own_band)
    parts = partners.reshape((2, 2) + partners.shape[1:])
    parts_x = pick(parts, 1 - part_low, 1)
    kept, passed, parts_x = together(kept, passed, parts_x)
    from_z = [swap(kept, 8), swap(passed, 12), swap(passed, 4)]
    parts, parts_x = pick(parts, part_low, 1), swap(parts_x, 2)
    kept_near = jnp.stack([pick(parts, part_half), pick(parts_x, part_half)])
    leaving = jnp.stack([pick(parts, 1 - part_half), pick(parts_x, 1 - part_half)])
    kept_near, leaving, *from_z = together(kept_near, leaving, *from_z)
    got_near, kept_far = swap(leaving, 8), swap(kept_near, 4)
    bands = jnp.stack([kept, from_z[2], from_z[0], from_z[1]])
    bands_x = swap(bands, 2)
    first, second = across(bands, 0, False), across(bands, 1, False)
    bands_x, first, second, got_near, kept_far = together(
        bands_x, first, second, got_near, kept_far
    )
    first_x, second_x = swap_away(first, 2), across(bands_x, 1, False)
    got_far = swap(got_near, 4)
    parts = [kept_near, kept_far, got_near]
    parts_c = [
        pltpu.with_memory_space_constraint(swap(part, 1), pltpu.HBM) for part in parts
    ]
    first = jnp.where(at_home, bands, first)
    early = [first, None, second, None] + parts + [None] + parts_c + [None]
    field_early = gather_part(right, left, early, EARLY)
    got_far, first_x, second_x, field_early = together(got_far, first_x, second_x, field_early)
    pieces = [first, first_x, second, second_x] + parts + [got_far] + parts_c + [swap(got_far, 1)]
    field_early, outs = late_part(
        right, left, z_left, z_back, square, field_early, bands_x, pieces, LATE, groups
    )
    got_far = outs[7] + swap(outs[11], 1)
    got_far, field_early = together(got_far, field_early)
    got_near = swap(got_far, 4)
    first = swap_away(outs[1], 2)
    bands_x = across(outs[3], 1, True) + jnp.where(at_home, outs[1], 0.0)
    outs = scatter_part(right, left, field_early, pieces, EARLY, outs)
    names = sorted(outs)
    first, bands_x, *blocks = together(first, bands_x, *[outs[name] for name in names])
    outs = dict(zip(names, blocks))
    got_near = got_near + outs[6] + swap(outs[10], 1)
    kept_far = outs[5] + swap(outs[9], 1)
    kept_near = outs[4] + swap(outs[8], 1)
    first, second = outs[0] + first, outs[2]
    leaving = swap(got_near, 8)
    kept_near = kept_near + swap(kept_far, 4)
    terms = [across(first, 0, True), across(second, 1, True), swap(bands_x, 2)]
    terms.append(jnp.where(at_home, first, 0.0))
    kept_near, leaving, *terms = together(kept_near, leaving, *terms)
    bands = [sum(term[z] for term in terms) for z in range(4)]
    kept_near, leaving, *bands = together(kept_near, leaving, *bands)
    from_z = [swap(bands[2], 8), swap(bands[3], 12), swap(bands[1], 4)]
    parts_x = swap(ordered(part_half, kept_near[1], leaving[1]), 2)
    parts = ordered(part_low, ordered(part_half, kept_near[0], leaving[0]), parts_x, 1)
    parts, *from_z = together(parts.reshape(partners.shape), *from_z)
    own_out = ordered(own_band, bands[0], from_z[1]) + ordered(own_band, from_z[0], from_z[2])
    return own_out, parts


def solution(mesh):
    groups, slabs = mesh.shape["band"], mesh.shape["slab"]
    spec = P("band", "slab", None, None)

    def shards(own, partners):
        if slabs == 16 and own.shape[0] == 2 and partners.shape[0] == 4 and STEPS == 2:
            return whole_fields(own, partners, groups, slabs)
        return pencils(own, partners, groups, slabs)

    return jax.shard_map(
        shards, mesh=mesh, in_specs=(spec, spec), out_specs=(spec, spec), check_vma=False
    )
```

```python
import functools
import math

import jax
import jax.numpy as jnp
import ml_dtypes
import numpy as np
from jax import lax
from jax.experimental import pallas as pl
from jax.experimental.pallas import tpu as pltpu
from jax.sharding import PartitionSpec as P

STEPS = 2


coulomb_scale = 46.9 * 46.9 / math.pi
precision = lax.Precision.HIGH


def cas_table(length):
    half = length // 2
    angles = np.arange(half) * (2.0 * math.pi / length)
    first = (np.cos(angles) + np.sin(angles)).astype(np.float32)
    wave = np.concatenate([first, -first])
    positions = np.arange(length)
    return wave[(positions[:, None] * positions[None, :]) % length]


def apply_table(pattern, field, table):
    return jnp.einsum(pattern, field, table, precision=precision)


def frequency(positions, length):
    return jnp.where(positions < length // 2, positions, positions - length).astype(jnp.float32)


def coulomb(z_waves, y_waves, x_waves, cells):
    square = (
        z_waves[:, None, None] * z_waves[:, None, None]
        + y_waves[None, :, None] * y_waves[None, :, None]
        + x_waves[None, None, :] * x_waves[None, None, :]
    )
    return jnp.where(square > 0, (coulomb_scale / float(cells)) / jnp.maximum(square, 1.0), 0.0)


def band_shift(block, groups, distance):
    if distance % groups == 0:
        return block
    route = [((b + distance) % groups, b) for b in range(groups)]
    return lax.ppermute(block, "band", route)


def pencils(own, partners, groups, slabs):
    length = own.shape[3]
    own_count, part_count = own.shape[0], partners.shape[0]
    table = jnp.asarray(cas_table(length))
    rows_y = length // slabs
    waves = frequency(lax.iota(jnp.int32, length), length)
    y_waves = frequency(
        lax.axis_index("slab") * rows_y + lax.iota(jnp.int32, rows_y), length
    )
    kernel = coulomb(waves, y_waves, waves, length**3)
    own_acc = jnp.zeros(own.shape, jnp.float32)
    part_acc = jnp.zeros(partners.shape, jnp.float32)
    for step_no in sorted(range(1, STEPS + 1), key=lambda s: s % groups != 0):
        bands = band_shift(own, groups, step_no)
        field = (bands[:, None] * partners[None]).reshape((-1,) + own.shape[1:])
        field = apply_table("pzyx,xk->pzyk", field, table)
        field = apply_table("pzyx,yk->pzkx", field, table)
        field = lax.all_to_all(field, "slab", split_axis=2, concat_axis=1, tiled=True)
        field = apply_table("pzyx,zk->pkyx", field, table) * kernel
        field = apply_table("pzyx,zk->pkyx", field, table)
        field = lax.all_to_all(field, "slab", split_axis=1, concat_axis=2, tiled=True)
        field = apply_table("pzyx,yk->pzkx", field, table)
        field = apply_table("pzyx,xk->pzyk", field, table)
        potential = field.reshape((own_count, part_count) + own.shape[1:])
        part_acc = part_acc + jnp.sum(potential * bands[:, None], axis=0)
        own_add = jnp.sum(potential * partners[None], axis=1)
        own_acc = own_acc + band_shift(own_add, groups, -step_no)
    return own_acc, part_acc


def two_terms(values):
    high = values.astype(jnp.bfloat16)
    return high, (values - high.astype(jnp.float32)).astype(jnp.bfloat16)


def table_terms(length):
    table = cas_table(length)
    high = table.astype(ml_dtypes.bfloat16)
    low = (table - high.astype(np.float32)).astype(ml_dtypes.bfloat16)
    return high, low


def from_left(high, low, xp=np):
    return xp.concatenate([xp.concatenate([high, high], 1), xp.concatenate([low, low], 1)], 0)


def product(left, right):
    return jnp.dot(left, right, preferred_element_type=jnp.float32)


def along_x(rows, right):
    high, low = two_terms(rows)
    both = product(jnp.concatenate([high, low], 1), right)
    return both[:, : both.shape[1] // 2] + both[:, both.shape[1] // 2 :]


def along_y(columns, left):
    high, low = two_terms(columns)
    both = product(left, jnp.concatenate([high, low], 0))
    return both[: both.shape[0] // 2] + both[both.shape[0] // 2 :]


def steps_of(late):
    steps = []
    for core in range(2):
        for x, z in [(1, 0), (1, 1), (1, 2), (0, 3), (1, 3)] if late else [(0, 0), (0, 1), (0, 2)]:
            steps.append((2 * core + x, z, 4 + 4 * core + z, x))
    return steps


EARLY, LATE = steps_of(False), steps_of(True)


def slabs_of(steps):
    return [(z >> 1) * 8 + (z & 1) * 4 + x * 2 + own // 2 for own, z, part, x in steps]


def used(steps):
    return sorted({step[0] for step in steps} | {step[2] for step in steps})


def to_field(pair_ref, out_ref, right, left):
    rows, length = pair_ref.shape[0], pair_ref.shape[1]
    for r in range(0, rows, 2):
        block = along_x(pair_ref[pl.ds(r, 2)].reshape(2 * length, length), right)
        block = along_y(jnp.concatenate([block[:length], block[length:]], 1), left)
        out_ref[pl.ds(r, length, stride=rows), :] = block[:, :length]
        out_ref[pl.ds(r + 1, length, stride=rows), :] = block[:, length:]


def from_field(field_ref, pot_ref, right, left):
    rows, length = pot_ref.shape[0], pot_ref.shape[1]
    for r in range(0, rows, 2):
        block = jnp.concatenate(
            [field_ref[pl.ds(r + k, length, stride=rows), :] for k in range(2)], 1
        )
        block = along_y(block, left)
        block = jnp.concatenate([block[:, :length], block[:, length:]], 0)
        pot_ref[pl.ds(r, 2)] = along_x(block, right).reshape(2, length, length)


def make_pairs(steps, turn, pieces, pair_ref):
    for k, (own, _, part, _) in enumerate(steps):

        @pl.when(turn == k)
        def _(own=own, part=part):
            pair_ref[...] = pieces[own][0] * pieces[part][0]


def make_terms(steps, turn, pieces, outs, pot_ref):
    for k, (own, _, part, _) in enumerate(steps):

        @pl.when(turn == k)
        def _(own=own, part=part):
            outs[own][0] = pot_ref[...] * pieces[part][0]
            outs[part][0] = pot_ref[...] * pieces[own][0]


def gather_kernel(steps, right_ref, left_ref, *refs):
    pieces, out_ref, pair_ref = dict(zip(used(steps), refs)), refs[-2], refs[-1]
    make_pairs(steps, pl.program_id(0), pieces, pair_ref)
    rows, length = pair_ref.shape[0], pair_ref.shape[1]
    to_field(pair_ref, out_ref.reshape(rows * length, length), right_ref[...], left_ref[...])


def late_kernel(
    steps, groups, right_ref, left_ref, z_left_ref, z_back_ref, square_ref, early_ref, home_ref,
    *refs,
):
    names = used(steps)
    pieces, early_out = dict(zip(names, refs)), refs[len(names)]
    outs = dict(zip(names, refs[len(names) + 1 :]))
    own_ref, part_ref, field_ref, middle_ref, in_sems, out_sems, middle_sems = refs[-7:]
    rows, length = own_ref.shape[1], own_ref.shape[2]
    count, part = len(steps), middle_ref.shape[1]

    def blocks(k, arrays):
        own, z, part, x = steps[k]
        return [(arrays[own].at[z], own_ref.at[k]), (arrays[part].at[x], part_ref.at[k])]

    def fetch(turns, arrays):
        for k in turns:
            for j, (block, held) in enumerate(blocks(k, arrays)):
                pltpu.make_async_copy(block, held, in_sems.at[j, k]).start()

    chosen = [k for k in range(count) if steps[k][0] == 1]
    at_home = lax.rem(lax.rem(lax.axis_index("slab"), 2) + 1, groups) == 0

    @pl.when(at_home)
    def _():
        fetch(chosen, {**pieces, 1: home_ref})

    @pl.when(jnp.logical_not(at_home))
    def _():
        fetch(chosen, pieces)

    fetch([k for k in range(count) if k not in chosen], pieces)
    middle_in = pltpu.make_async_copy(early_ref, middle_ref, middle_sems.at[0])
    middle_in.start()

    @pl.loop(0, count, unroll=5)
    def _(k):
        pltpu.make_async_copy(pieces[names[0]].at[0], own_ref.at[k], in_sems.at[0, k]).wait()
        pltpu.make_async_copy(pieces[names[0]].at[0], part_ref.at[k], in_sems.at[1, k]).wait()
        out_ref = field_ref.at[k]
        for r in range(0, rows, 2):
            pair = own_ref[k, pl.ds(r, 2)] * part_ref[k, pl.ds(r, 2)]
            block = along_x(pair.reshape(2 * length, length), right_ref[...])
            block = along_y(
                jnp.concatenate([block[:length], block[length:]], 1), left_ref[...]
            )
            out_ref[pl.ds(r, length, stride=rows), :] = block[:, :length]
            out_ref[pl.ds(r + 1, length, stride=rows), :] = block[:, length:]

    middle_in.wait()
    group = 32
    scale = coulomb_scale / float(length**3)

    @pl.loop(0, length // group)
    def _(i):
        for k in range(0, group, 2):
            columns, factors, spans = [], [], []
            for j in range(2):
                y = i * group + k + j
                spans.append(pl.ds(pl.multiple_of(y * rows, rows), rows))
                late = field_ref[:, spans[j], :].reshape(count * rows, length)
                columns.append(jnp.concatenate([middle_ref[y], late], 0))
                wave = frequency(y, length)
                total = square_ref[...] + wave * wave
                factors.append(jnp.where(total > 0, scale / jnp.maximum(total, 1.0), 0.0))
            block = along_y(jnp.concatenate(columns, 1), z_left_ref[...])
            block = along_y(block * jnp.concatenate(factors, 1), z_back_ref[...])
            for j in range(2):
                piece = block[:, j * length : (j + 1) * length]
                middle_ref[i * group + k + j] = piece[:part]
                field_ref[:, spans[j], :] = piece[part:].reshape(count, rows, length)

    middle_out = pltpu.make_async_copy(middle_ref, early_out, middle_sems.at[1])
    middle_out.start()

    @pl.loop(0, count, unroll=5)
    def _(k):
        in_ref = field_ref.at[k]
        for r in range(0, rows, 2):
            block = jnp.concatenate(
                [in_ref[pl.ds(r + j, length, stride=rows), :] for j in range(2)], 1
            )
            block = along_y(block, left_ref[...])
            block = jnp.concatenate([block[:, :length], block[:, length:]], 0)
            block = along_x(block, right_ref[...]).reshape(2, length, length)
            span = pl.ds(r, 2)
            own_term = block * part_ref[k, span]
            part_ref[k, span] = block * own_ref[k, span]
            own_ref[k, span] = own_term
        for turn in range(count):

            @pl.when(k == turn)
            def _(turn=turn):
                for j, (block, held) in enumerate(blocks(turn, outs)):
                    pltpu.make_async_copy(held, block, out_sems.at[j, turn]).start()

    for k in range(count):
        for j, (block, held) in enumerate(blocks(k, outs)):
            pltpu.make_async_copy(held, block, out_sems.at[j, k]).wait()
    middle_out.wait()


def scatter_kernel(steps, right_ref, left_ref, field_ref, *refs):
    names = used(steps)
    pieces, outs = dict(zip(names, refs)), dict(zip(names, refs[-1 - len(names) : -1]))
    pot_ref = refs[-1]
    rows, length = pot_ref.shape[0], pot_ref.shape[1]
    flat = field_ref.reshape(rows * length, length)
    from_field(flat, pot_ref, right_ref[...], left_ref[...])
    make_terms(steps, pl.program_id(0), pieces, outs, pot_ref)


def piece_specs(steps, rows, length, starts=(0,)):
    def spec(name):
        visits = []
        for start in starts:
            for turn, (own, z, part, x) in enumerate(steps):
                if name in (own, part):
                    visits.append((start + turn, z if name == own else x))

        def index(i):
            block = visits[0][1]
            for (_, before), (turn, after) in zip(visits, visits[1:]):
                block = block + jnp.where(i >= turn, after - before, 0)
            return (block, 0, 0, 0)

        return pl.BlockSpec((1, rows, length, length), index)

    return [spec(name) for name in used(steps)]


def fixed_spec(shape):
    return pl.BlockSpec(shape, lambda i: (0,) * len(shape))


def settings(megabytes):
    return pltpu.CompilerParams(
        dimension_semantics=("arbitrary",), vmem_limit_bytes=megabytes * 2**20
    )


def cost(cells, length, fields, transforms):
    return pl.CostEstimate(
        flops=transforms * 8 * cells * length, bytes_accessed=4 * fields * cells, transcendentals=0
    )


def gather_part(right, left, pieces, steps):
    rows, length = pieces[0].shape[1], pieces[0].shape[2]
    count = len(steps)
    return pl.pallas_call(
        functools.partial(gather_kernel, steps),
        grid=(count,),
        in_specs=[fixed_spec(right.shape), fixed_spec(left.shape)]
        + piece_specs(steps, rows, length),
        out_specs=pl.BlockSpec((length, rows, length), lambda i: (0, i, 0)),
        out_shape=jax.ShapeDtypeStruct((length, count * rows, length), jnp.float32),
        scratch_shapes=[pltpu.VMEM((rows, length, length), jnp.float32)],
        compiler_params=settings(20),
        cost_estimate=cost(count * rows * length * length, length, 3, 2),
    )(right, left, *[pieces[name] for name in used(steps)])


def late_part(right, left, z_left, z_back, square, early, home, pieces, steps, groups):
    rows, length = pieces[0].shape[1], pieces[0].shape[2]
    names = used(steps)
    count = len(steps)
    tables = [right, left, z_left, z_back, square]
    anywhere = pl.BlockSpec(memory_space=pl.ANY)
    early, *outs = pl.pallas_call(
        functools.partial(late_kernel, steps, groups),
        in_specs=[pl.BlockSpec(memory_space=pltpu.VMEM)] * len(tables)
        + [anywhere] * (2 + len(names)),
        out_specs=[anywhere] * (1 + len(names)),
        out_shape=[jax.ShapeDtypeStruct(early.shape, jnp.float32)]
        + [jax.ShapeDtypeStruct(pieces[name].shape, jnp.float32) for name in names],
        scratch_shapes=[
            pltpu.VMEM((count, rows, length, length), jnp.float32),
            pltpu.VMEM((count, rows, length, length), jnp.float32),
            pltpu.VMEM((count, rows * length, length), jnp.float32),
            pltpu.VMEM(early.shape, jnp.float32),
            pltpu.SemaphoreType.DMA((2, count)),
            pltpu.SemaphoreType.DMA((2, count)),
            pltpu.SemaphoreType.DMA((2,)),
        ],
        compiler_params=pltpu.CompilerParams(vmem_limit_bytes=32 * 2**20),
        cost_estimate=cost(length**3, length, 4, 5),
    )(*tables, early, home, *[pieces[name] for name in names])
    return early, dict(zip(names, outs))


def scatter_part(right, left, field, pieces, steps, held):
    rows, length = pieces[0].shape[1], pieces[0].shape[2]
    names = used(steps)
    specs = piece_specs(steps, rows, length)
    kept = [name for name in names if name in held]
    outs = pl.pallas_call(
        functools.partial(scatter_kernel, steps),
        grid=(len(steps),),
        in_specs=[
            fixed_spec(right.shape), fixed_spec(left.shape),
            pl.BlockSpec((length, rows, length), lambda i: (0, i, 0)),
        ]
        + specs
        + [pl.BlockSpec(memory_space=pl.ANY)] * len(kept),
        out_specs=specs,
        out_shape=[jax.ShapeDtypeStruct(pieces[name].shape, jnp.float32) for name in names],
        input_output_aliases={
            3 + len(names) + k: names.index(name) for k, name in enumerate(kept)
        },
        scratch_shapes=[pltpu.VMEM((rows, length, length), jnp.float32)],
        compiler_params=settings(32),
        cost_estimate=cost(len(steps) * rows * length * length, length, 5, 2),
    )(right, left, field, *[pieces[name] for name in names], *[held[name] for name in kept])
    return dict(zip(names, outs))


def whole_fields(own, partners, groups, slabs):
    length = own.shape[3]
    rows = own.shape[1]
    plane = own.shape[2:]
    me = lax.axis_index("slab")
    part_half, own_band, part_low = (me >> 3) & 1, (me >> 2) & 1, (me >> 1) & 1

    at_home = ((me & 1) + 1) % groups == 0

    def swap(block, mask):
        return lax.ppermute(block, "slab", [(i ^ mask, i) for i in range(slabs)])

    def swap_away(block, mask):
        away = [i for i in range(slabs) if ((i & 1) + 1) % groups != 0]
        return lax.ppermute(block, "slab", [(i ^ mask, i) for i in away])

    def across(block, flip, back):
        route = []
        for b in range(groups):
            for i in range(slabs):
                source = ((b + 1 + (i & 1)) % groups) * slabs + (i ^ flip)
                target = b * slabs + i
                if source != target:
                    route.append((target, source) if back else (source, target))
        return lax.ppermute(block, ("band", "slab"), route)

    def pick(block, position, axis=0):
        return lax.dynamic_index_in_dim(block, position, axis, keepdims=False)

    def ordered(position, mine, other, axis=0):
        shape = [1] * (mine.ndim + 1)
        shape[axis] = 2
        first = lax.iota(jnp.int32, 2).reshape(shape) == position
        return jnp.where(first, jnp.expand_dims(mine, axis), jnp.expand_dims(other, axis))

    def together(*blocks):
        return lax.optimization_barrier(blocks)

    high, low = table_terms(length)
    left = jnp.asarray(from_left(high, low))
    right = jnp.asarray(from_left(high, low).T)
    slab_of = me ^ jnp.asarray(np.array(slabs_of(EARLY) + slabs_of(LATE), np.int32))
    z_high, z_low = [
        jnp.take(jnp.asarray(term).reshape(slabs, rows, length), slab_of, axis=0).reshape(
            length, length
        )
        for term in (high, low)
    ]
    z_left, z_back = from_left(z_high.T, z_low.T, jnp), from_left(z_high, z_low, jnp)
    waves = frequency(lax.iota(jnp.int32, length), length)
    square = waves[:, None] * waves[:, None] + waves[None] * waves[None]

    kept, passed = pick(own, own_band), pick(own, 1 - own_band)
    parts = partners.reshape((2, 2) + partners.shape[1:])
    parts_x = pick(parts, 1 - part_low, 1)
    kept, passed, parts_x = together(kept, passed, parts_x)
    from_z = [swap(kept, 8), swap(passed, 12), swap(passed, 4)]
    parts, parts_x = pick(parts, part_low, 1), swap(parts_x, 2)
    kept_near = jnp.stack([pick(parts, part_half), pick(parts_x, part_half)])
    leaving = jnp.stack([pick(parts, 1 - part_half), pick(parts_x, 1 - part_half)])
    kept_near, leaving, *from_z = together(kept_near, leaving, *from_z)
    got_near, kept_far = swap(leaving, 8), swap(kept_near, 4)
    bands = jnp.stack([kept, from_z[2], from_z[0], from_z[1]])
    bands_x = swap(bands, 2)
    first, second = across(bands, 0, False), across(bands, 1, False)
    bands_x, first, second, got_near, kept_far = together(
        bands_x, first, second, got_near, kept_far
    )
    first_x, second_x = swap_away(first, 2), across(bands_x, 1, False)
    got_far = swap(got_near, 4)
    second = pltpu.with_memory_space_constraint(second, pltpu.HBM)
    parts = [kept_near, kept_far, got_near]
    parts_c = [
        pltpu.with_memory_space_constraint(swap(part, 1), pltpu.HBM) for part in parts
    ]
    first = jnp.where(at_home, bands, first)
    early = [first, None, second, None] + parts + [None] + parts_c + [None]
    field_early = gather_part(right, left, early, EARLY)
    got_far, first_x, second_x, field_early = together(got_far, first_x, second_x, field_early)
    pieces = [first, first_x, second, second_x] + parts + [got_far] + parts_c + [swap(got_far, 1)]
    field_early, outs = late_part(
        right, left, z_left, z_back, square, field_early, bands_x, pieces, LATE, groups
    )
    got_far = outs[7] + swap(outs[11], 1)
    got_far, field_early = together(got_far, field_early)
    got_near = swap(got_far, 4)
    first = swap_away(outs[1], 2)
    bands_x = across(outs[3], 1, True) + jnp.where(at_home, outs[1], 0.0)
    outs = scatter_part(right, left, field_early, pieces, EARLY, outs)
    names = sorted(outs)
    first, bands_x, *blocks = together(first, bands_x, *[outs[name] for name in names])
    outs = dict(zip(names, blocks))
    got_near = got_near + outs[6] + swap(outs[10], 1)
    kept_far = outs[5] + swap(outs[9], 1)
    kept_near = outs[4] + swap(outs[8], 1)
    first, second = outs[0] + first, outs[2]
    leaving = swap(got_near, 8)
    kept_near = kept_near + swap(kept_far, 4)
    terms = [across(first, 0, True), across(second, 1, True), swap(bands_x, 2)]
    terms.append(jnp.where(at_home, first, 0.0))
    kept_near, leaving, *terms = together(kept_near, leaving, *terms)
    bands = [sum(term[z] for term in terms) for z in range(4)]
    kept_near, leaving, *bands = together(kept_near, leaving, *bands)
    from_z = [swap(bands[2], 8), swap(bands[3], 12), swap(bands[1], 4)]
    parts_x = swap(ordered(part_half, kept_near[1], leaving[1]), 2)
    parts = ordered(part_low, ordered(part_half, kept_near[0], leaving[0]), parts_x, 1)
    parts, *from_z = together(parts.reshape(partners.shape), *from_z)
    own_out = ordered(own_band, bands[0], from_z[1]) + ordered(own_band, from_z[0], from_z[2])
    return own_out, parts


def solution(mesh):
    groups, slabs = mesh.shape["band"], mesh.shape["slab"]
    spec = P("band", "slab", None, None)

    def shards(own, partners):
        if slabs == 16 and own.shape[0] == 2 and partners.shape[0] == 4 and STEPS == 2:
            return whole_fields(own, partners, groups, slabs)
        return pencils(own, partners, groups, slabs)

    return jax.shard_map(
        shards, mesh=mesh, in_specs=(spec, spec), out_specs=(spec, spec), check_vma=False
    )
```

```python
import functools
import math

import jax
import jax.numpy as jnp
import ml_dtypes
import numpy as np
from jax import lax
from jax.experimental import pallas as pl
from jax.experimental.pallas import tpu as pltpu
from jax.sharding import PartitionSpec as P

STEPS = 2


coulomb_scale = 46.9 * 46.9 / math.pi
precision = lax.Precision.HIGH


def cas_table(length):
    half = length // 2
    angles = np.arange(half) * (2.0 * math.pi / length)
    first = (np.cos(angles) + np.sin(angles)).astype(np.float32)
    wave = np.concatenate([first, -first])
    positions = np.arange(length)
    return wave[(positions[:, None] * positions[None, :]) % length]


def apply_table(pattern, field, table):
    return jnp.einsum(pattern, field, table, precision=precision)


def frequency(positions, length):
    return jnp.where(positions < length // 2, positions, positions - length).astype(jnp.float32)


def coulomb(z_waves, y_waves, x_waves, cells):
    square = (
        z_waves[:, None, None] * z_waves[:, None, None]
        + y_waves[None, :, None] * y_waves[None, :, None]
        + x_waves[None, None, :] * x_waves[None, None, :]
    )
    return jnp.where(square > 0, (coulomb_scale / float(cells)) / jnp.maximum(square, 1.0), 0.0)


def band_shift(block, groups, distance):
    if distance % groups == 0:
        return block
    route = [((b + distance) % groups, b) for b in range(groups)]
    return lax.ppermute(block, "band", route)


def pencils(own, partners, groups, slabs):
    length = own.shape[3]
    own_count, part_count = own.shape[0], partners.shape[0]
    table = jnp.asarray(cas_table(length))
    rows_y = length // slabs
    waves = frequency(lax.iota(jnp.int32, length), length)
    y_waves = frequency(
        lax.axis_index("slab") * rows_y + lax.iota(jnp.int32, rows_y), length
    )
    kernel = coulomb(waves, y_waves, waves, length**3)
    own_acc = jnp.zeros(own.shape, jnp.float32)
    part_acc = jnp.zeros(partners.shape, jnp.float32)
    for step_no in sorted(range(1, STEPS + 1), key=lambda s: s % groups != 0):
        bands = band_shift(own, groups, step_no)
        field = (bands[:, None] * partners[None]).reshape((-1,) + own.shape[1:])
        field = apply_table("pzyx,xk->pzyk", field, table)
        field = apply_table("pzyx,yk->pzkx", field, table)
        field = lax.all_to_all(field, "slab", split_axis=2, concat_axis=1, tiled=True)
        field = apply_table("pzyx,zk->pkyx", field, table) * kernel
        field = apply_table("pzyx,zk->pkyx", field, table)
        field = lax.all_to_all(field, "slab", split_axis=1, concat_axis=2, tiled=True)
        field = apply_table("pzyx,yk->pzkx", field, table)
        field = apply_table("pzyx,xk->pzyk", field, table)
        potential = field.reshape((own_count, part_count) + own.shape[1:])
        part_acc = part_acc + jnp.sum(potential * bands[:, None], axis=0)
        own_add = jnp.sum(potential * partners[None], axis=1)
        own_acc = own_acc + band_shift(own_add, groups, -step_no)
    return own_acc, part_acc


def two_terms(values):
    high = values.astype(jnp.bfloat16)
    return high, (values - high.astype(jnp.float32)).astype(jnp.bfloat16)


def table_terms(length):
    table = cas_table(length)
    high = table.astype(ml_dtypes.bfloat16)
    low = (table - high.astype(np.float32)).astype(ml_dtypes.bfloat16)
    return high, low


def from_left(high, low, xp=np):
    return xp.concatenate([xp.concatenate([high, high], 1), xp.concatenate([low, low], 1)], 0)


def product(left, right):
    return jnp.dot(left, right, preferred_element_type=jnp.float32)


def along_x(rows, right):
    high, low = two_terms(rows)
    both = product(jnp.concatenate([high, low], 1), right)
    return both[:, : both.shape[1] // 2] + both[:, both.shape[1] // 2 :]


def along_y(columns, left):
    high, low = two_terms(columns)
    both = product(left, jnp.concatenate([high, low], 0))
    return both[: both.shape[0] // 2] + both[both.shape[0] // 2 :]


def steps_of(late):
    steps = []
    for core in range(2):
        for x, z in [(1, 0), (1, 1), (1, 2), (0, 3), (1, 3)] if late else [(0, 0), (0, 1), (0, 2)]:
            steps.append((2 * core + x, z, 4 + 4 * core + z, x))
    return steps


EARLY, LATE = steps_of(False), steps_of(True)


def slabs_of(steps):
    return [(z >> 1) * 8 + (z & 1) * 4 + x * 2 + own // 2 for own, z, part, x in steps]


def used(steps):
    return sorted({step[0] for step in steps} | {step[2] for step in steps})


def to_field(pair_ref, out_ref, right, left):
    rows, length = pair_ref.shape[0], pair_ref.shape[1]
    for r in range(0, rows, 2):
        block = along_x(pair_ref[pl.ds(r, 2)].reshape(2 * length, length), right)
        block = along_y(jnp.concatenate([block[:length], block[length:]], 1), left)
        out_ref[pl.ds(r, length, stride=rows), :] = block[:, :length]
        out_ref[pl.ds(r + 1, length, stride=rows), :] = block[:, length:]


def from_field(field_ref, pot_ref, right, left):
    rows, length = pot_ref.shape[0], pot_ref.shape[1]
    for r in range(0, rows, 2):
        block = jnp.concatenate(
            [field_ref[pl.ds(r + k, length, stride=rows), :] for k in range(2)], 1
        )
        block = along_y(block, left)
        block = jnp.concatenate([block[:, :length], block[:, length:]], 0)
        pot_ref[pl.ds(r, 2)] = along_x(block, right).reshape(2, length, length)


def make_pairs(steps, turn, pieces, pair_ref):
    for k, (own, _, part, _) in enumerate(steps):

        @pl.when(turn == k)
        def _(own=own, part=part):
            pair_ref[...] = pieces[own][0] * pieces[part][0]


def make_terms(steps, turn, pieces, outs, pot_ref):
    for k, (own, _, part, _) in enumerate(steps):

        @pl.when(turn == k)
        def _(own=own, part=part):
            outs[own][0] = pot_ref[...] * pieces[part][0]
            outs[part][0] = pot_ref[...] * pieces[own][0]


def gather_kernel(steps, right_ref, left_ref, *refs):
    pieces, out_ref, pair_ref = dict(zip(used(steps), refs)), refs[-2], refs[-1]
    make_pairs(steps, pl.program_id(0), pieces, pair_ref)
    rows, length = pair_ref.shape[0], pair_ref.shape[1]
    to_field(pair_ref, out_ref.reshape(rows * length, length), right_ref[...], left_ref[...])


def late_kernel(
    steps, groups, right_ref, left_ref, z_left_ref, z_back_ref, square_ref, early_ref, home_ref,
    *refs,
):
    names = used(steps)
    pieces, early_out = dict(zip(names, refs)), refs[len(names)]
    outs = dict(zip(names, refs[len(names) + 1 :]))
    own_ref, part_ref, field_ref, middle_ref, in_sems, out_sems, middle_sems = refs[-7:]
    rows, length = own_ref.shape[1], own_ref.shape[2]
    count, part = len(steps), middle_ref.shape[1]

    def blocks(k, arrays):
        own, z, part, x = steps[k]
        return [(arrays[own].at[z], own_ref.at[k]), (arrays[part].at[x], part_ref.at[k])]

    def fetch(turns, arrays):
        for k in turns:
            for j, (block, held) in enumerate(blocks(k, arrays)):
                pltpu.make_async_copy(block, held, in_sems.at[j, k]).start()

    chosen = [k for k in range(count) if steps[k][0] == 1]
    at_home = lax.rem(lax.rem(lax.axis_index("slab"), 2) + 1, groups) == 0

    @pl.when(at_home)
    def _():
        fetch(chosen, {**pieces, 1: home_ref})

    @pl.when(jnp.logical_not(at_home))
    def _():
        fetch(chosen, pieces)

    fetch([k for k in range(count) if k not in chosen], pieces)
    middle_in = pltpu.make_async_copy(early_ref, middle_ref, middle_sems.at[0])
    middle_in.start()

    @pl.loop(0, count, unroll=10)
    def _(k):
        pltpu.make_async_copy(pieces[names[0]].at[0], own_ref.at[k], in_sems.at[0, k]).wait()
        pltpu.make_async_copy(pieces[names[0]].at[0], part_ref.at[k], in_sems.at[1, k]).wait()
        out_ref = field_ref.at[k]
        for r in range(0, rows, 2):
            pair = own_ref[k, pl.ds(r, 2)] * part_ref[k, pl.ds(r, 2)]
            block = along_x(pair.reshape(2 * length, length), right_ref[...])
            block = along_y(
                jnp.concatenate([block[:length], block[length:]], 1), left_ref[...]
            )
            out_ref[pl.ds(r, length, stride=rows), :] = block[:, :length]
            out_ref[pl.ds(r + 1, length, stride=rows), :] = block[:, length:]

    middle_in.wait()
    group = 64
    scale = coulomb_scale / float(length**3)

    @pl.loop(0, length // group)
    def _(i):
        for k in range(0, group, 2):
            columns, factors, spans = [], [], []
            for j in range(2):
                y = i * group + k + j
                spans.append(pl.ds(pl.multiple_of(y * rows, rows), rows))
                late = field_ref[:, spans[j], :].reshape(count * rows, length)
                columns.append(jnp.concatenate([middle_ref[y], late], 0))
                wave = frequency(y, length)
                total = square_ref[...] + wave * wave
                factors.append(jnp.where(total > 0, scale / jnp.maximum(total, 1.0), 0.0))
            block = along_y(jnp.concatenate(columns, 1), z_left_ref[...])
            block = along_y(block * jnp.concatenate(factors, 1), z_back_ref[...])
            for j in range(2):
                piece = block[:, j * length : (j + 1) * length]
                middle_ref[i * group + k + j] = piece[:part]
                field_ref[:, spans[j], :] = piece[part:].reshape(count, rows, length)

    middle_out = pltpu.make_async_copy(middle_ref, early_out, middle_sems.at[1])
    middle_out.start()

    @pl.loop(0, count, unroll=10)
    def _(k):
        in_ref = field_ref.at[k]
        for r in range(0, rows, 2):
            block = jnp.concatenate(
                [in_ref[pl.ds(r + j, length, stride=rows), :] for j in range(2)], 1
            )
            block = along_y(block, left_ref[...])
            block = jnp.concatenate([block[:, :length], block[:, length:]], 0)
            block = along_x(block, right_ref[...]).reshape(2, length, length)
            span = pl.ds(r, 2)
            own_term = block * part_ref[k, span]
            part_ref[k, span] = block * own_ref[k, span]
            own_ref[k, span] = own_term
        for turn in range(count):

            @pl.when(k == turn)
            def _(turn=turn):
                for j, (block, held) in enumerate(blocks(turn, outs)):
                    pltpu.make_async_copy(held, block, out_sems.at[j, turn]).start()

    for k in range(count):
        for j, (block, held) in enumerate(blocks(k, outs)):
            pltpu.make_async_copy(held, block, out_sems.at[j, k]).wait()
    middle_out.wait()


def scatter_kernel(steps, right_ref, left_ref, field_ref, *refs):
    names = used(steps)
    pieces, outs = dict(zip(names, refs)), dict(zip(names, refs[-1 - len(names) : -1]))
    pot_ref = refs[-1]
    rows, length = pot_ref.shape[0], pot_ref.shape[1]
    flat = field_ref.reshape(rows * length, length)
    from_field(flat, pot_ref, right_ref[...], left_ref[...])
    make_terms(steps, pl.program_id(0), pieces, outs, pot_ref)


def piece_specs(steps, rows, length, starts=(0,)):
    def spec(name):
        visits = []
        for start in starts:
            for turn, (own, z, part, x) in enumerate(steps):
                if name in (own, part):
                    visits.append((start + turn, z if name == own else x))

        def index(i):
            block = visits[0][1]
            for (_, before), (turn, after) in zip(visits, visits[1:]):
                block = block + jnp.where(i >= turn, after - before, 0)
            return (block, 0, 0, 0)

        return pl.BlockSpec((1, rows, length, length), index)

    return [spec(name) for name in used(steps)]


def fixed_spec(shape):
    return pl.BlockSpec(shape, lambda i: (0,) * len(shape))


def settings(megabytes):
    return pltpu.CompilerParams(
        dimension_semantics=("arbitrary",), vmem_limit_bytes=megabytes * 2**20
    )


def cost(cells, length, fields, transforms):
    return pl.CostEstimate(
        flops=transforms * 8 * cells * length, bytes_accessed=4 * fields * cells, transcendentals=0
    )


def gather_part(right, left, pieces, steps):
    rows, length = pieces[0].shape[1], pieces[0].shape[2]
    count = len(steps)
    return pl.pallas_call(
        functools.partial(gather_kernel, steps),
        grid=(count,),
        in_specs=[fixed_spec(right.shape), fixed_spec(left.shape)]
        + piece_specs(steps, rows, length),
        out_specs=pl.BlockSpec((length, rows, length), lambda i: (0, i, 0)),
        out_shape=jax.ShapeDtypeStruct((length, count * rows, length), jnp.float32),
        scratch_shapes=[pltpu.VMEM((rows, length, length), jnp.float32)],
        compiler_params=settings(20),
        cost_estimate=cost(count * rows * length * length, length, 3, 2),
    )(right, left, *[pieces[name] for name in used(steps)])


def late_part(right, left, z_left, z_back, square, early, home, pieces, steps, groups):
    rows, length = pieces[0].shape[1], pieces[0].shape[2]
    names = used(steps)
    count = len(steps)
    tables = [right, left, z_left, z_back, square]
    anywhere = pl.BlockSpec(memory_space=pl.ANY)
    early, *outs = pl.pallas_call(
        functools.partial(late_kernel, steps, groups),
        in_specs=[pl.BlockSpec(memory_space=pltpu.VMEM)] * len(tables)
        + [anywhere] * (2 + len(names)),
        out_specs=[anywhere] * (1 + len(names)),
        out_shape=[jax.ShapeDtypeStruct(early.shape, jnp.float32)]
        + [jax.ShapeDtypeStruct(pieces[name].shape, jnp.float32) for name in names],
        scratch_shapes=[
            pltpu.VMEM((count, rows, length, length), jnp.float32),
            pltpu.VMEM((count, rows, length, length), jnp.float32),
            pltpu.VMEM((count, rows * length, length), jnp.float32),
            pltpu.VMEM(early.shape, jnp.float32),
            pltpu.SemaphoreType.DMA((2, count)),
            pltpu.SemaphoreType.DMA((2, count)),
            pltpu.SemaphoreType.DMA((2,)),
        ],
        compiler_params=pltpu.CompilerParams(vmem_limit_bytes=32 * 2**20),
        cost_estimate=cost(length**3, length, 4, 5),
    )(*tables, early, home, *[pieces[name] for name in names])
    return early, dict(zip(names, outs))


def scatter_part(right, left, field, pieces, steps, held):
    rows, length = pieces[0].shape[1], pieces[0].shape[2]
    names = used(steps)
    specs = piece_specs(steps, rows, length)
    kept = [name for name in names if name in held]
    outs = pl.pallas_call(
        functools.partial(scatter_kernel, steps),
        grid=(len(steps),),
        in_specs=[
            fixed_spec(right.shape), fixed_spec(left.shape),
            pl.BlockSpec((length, rows, length), lambda i: (0, i, 0)),
        ]
        + specs
        + [pl.BlockSpec(memory_space=pl.ANY)] * len(kept),
        out_specs=specs,
        out_shape=[jax.ShapeDtypeStruct(pieces[name].shape, jnp.float32) for name in names],
        input_output_aliases={
            3 + len(names) + k: names.index(name) for k, name in enumerate(kept)
        },
        scratch_shapes=[pltpu.VMEM((rows, length, length), jnp.float32)],
        compiler_params=settings(32),
        cost_estimate=cost(len(steps) * rows * length * length, length, 5, 2),
    )(right, left, field, *[pieces[name] for name in names], *[held[name] for name in kept])
    return dict(zip(names, outs))


def whole_fields(own, partners, groups, slabs):
    length = own.shape[3]
    rows = own.shape[1]
    plane = own.shape[2:]
    me = lax.axis_index("slab")
    part_half, own_band, part_low = (me >> 3) & 1, (me >> 2) & 1, (me >> 1) & 1

    at_home = ((me & 1) + 1) % groups == 0

    def swap(block, mask):
        return lax.ppermute(block, "slab", [(i ^ mask, i) for i in range(slabs)])

    def swap_away(block, mask):
        away = [i for i in range(slabs) if ((i & 1) + 1) % groups != 0]
        return lax.ppermute(block, "slab", [(i ^ mask, i) for i in away])

    def across(block, flip, back):
        route = []
        for b in range(groups):
            for i in range(slabs):
                source = ((b + 1 + (i & 1)) % groups) * slabs + (i ^ flip)
                target = b * slabs + i
                if source != target:
                    route.append((target, source) if back else (source, target))
        return lax.ppermute(block, ("band", "slab"), route)

    def pick(block, position, axis=0):
        return lax.dynamic_index_in_dim(block, position, axis, keepdims=False)

    def ordered(position, mine, other, axis=0):
        shape = [1] * (mine.ndim + 1)
        shape[axis] = 2
        first = lax.iota(jnp.int32, 2).reshape(shape) == position
        return jnp.where(first, jnp.expand_dims(mine, axis), jnp.expand_dims(other, axis))

    def together(*blocks):
        return lax.optimization_barrier(blocks)

    high, low = table_terms(length)
    left = jnp.asarray(from_left(high, low))
    right = jnp.asarray(from_left(high, low).T)
    slab_of = me ^ jnp.asarray(np.array(slabs_of(EARLY) + slabs_of(LATE), np.int32))
    z_high, z_low = [
        jnp.take(jnp.asarray(term).reshape(slabs, rows, length), slab_of, axis=0).reshape(
            length, length
        )
        for term in (high, low)
    ]
    z_left, z_back = from_left(z_high.T, z_low.T, jnp), from_left(z_high, z_low, jnp)
    waves = frequency(lax.iota(jnp.int32, length), length)
    square = waves[:, None] * waves[:, None] + waves[None] * waves[None]

    kept, passed = pick(own, own_band), pick(own, 1 - own_band)
    parts = partners.reshape((2, 2) + partners.shape[1:])
    parts_x = pick(parts, 1 - part_low, 1)
    kept, passed, parts_x = together(kept, passed, parts_x)
    from_z = [swap(kept, 8), swap(passed, 12), swap(passed, 4)]
    parts, parts_x = pick(parts, part_low, 1), swap(parts_x, 2)
    kept_near = jnp.stack([pick(parts, part_half), pick(parts_x, part_half)])
    leaving = jnp.stack([pick(parts, 1 - part_half), pick(parts_x, 1 - part_half)])
    kept_near, leaving, *from_z = together(kept_near, leaving, *from_z)
    got_near, kept_far = swap(leaving, 8), swap(kept_near, 4)
    bands = jnp.stack([kept, from_z[2], from_z[0], from_z[1]])
    bands_x = swap(bands, 2)
    first, second = across(bands, 0, False), across(bands, 1, False)
    bands_x, first, second, got_near, kept_far = together(
        bands_x, first, second, got_near, kept_far
    )
    first_x, second_x = swap_away(first, 2), across(bands_x, 1, False)
    got_far = swap(got_near, 4)
    second = pltpu.with_memory_space_constraint(second, pltpu.HBM)
    parts = [kept_near, kept_far, got_near]
    parts_c = [
        pltpu.with_memory_space_constraint(swap(part, 1), pltpu.HBM) for part in parts
    ]
    first = jnp.where(at_home, bands, first)
    early = [first, None, second, None] + parts + [None] + parts_c + [None]
    field_early = gather_part(right, left, early, EARLY)
    got_far, first_x, second_x, field_early = together(got_far, first_x, second_x, field_early)
    pieces = [first, first_x, second, second_x] + parts + [got_far] + parts_c + [swap(got_far, 1)]
    field_early, outs = late_part(
        right, left, z_left, z_back, square, field_early, bands_x, pieces, LATE, groups
    )
    got_far = outs[7] + swap(outs[11], 1)
    got_far, field_early = together(got_far, field_early)
    got_near = swap(got_far, 4)
    first = swap_away(outs[1], 2)
    bands_x = across(outs[3], 1, True) + jnp.where(at_home, outs[1], 0.0)
    outs = scatter_part(right, left, field_early, pieces, EARLY, outs)
    names = sorted(outs)
    first, bands_x, *blocks = together(first, bands_x, *[outs[name] for name in names])
    outs = dict(zip(names, blocks))
    got_near = got_near + outs[6] + swap(outs[10], 1)
    kept_far = outs[5] + swap(outs[9], 1)
    kept_near = outs[4] + swap(outs[8], 1)
    first, second = outs[0] + first, outs[2]
    leaving = swap(got_near, 8)
    kept_near = kept_near + swap(kept_far, 4)
    terms = [across(first, 0, True), across(second, 1, True), swap(bands_x, 2)]
    terms.append(jnp.where(at_home, first, 0.0))
    kept_near, leaving, *terms = together(kept_near, leaving, *terms)
    bands = [sum(term[z] for term in terms) for z in range(4)]
    kept_near, leaving, *bands = together(kept_near, leaving, *bands)
    from_z = [swap(bands[2], 8), swap(bands[3], 12), swap(bands[1], 4)]
    parts_x = swap(ordered(part_half, kept_near[1], leaving[1]), 2)
    parts = ordered(part_low, ordered(part_half, kept_near[0], leaving[0]), parts_x, 1)
    parts, *from_z = together(parts.reshape(partners.shape), *from_z)
    own_out = ordered(own_band, bands[0], from_z[1]) + ordered(own_band, from_z[0], from_z[2])
    return own_out, parts


def solution(mesh):
    groups, slabs = mesh.shape["band"], mesh.shape["slab"]
    spec = P("band", "slab", None, None)

    def shards(own, partners):
        if slabs == 16 and own.shape[0] == 2 and partners.shape[0] == 4 and STEPS == 2:
            return whole_fields(own, partners, groups, slabs)
        return pencils(own, partners, groups, slabs)

    return jax.shard_map(
        shards, mesh=mesh, in_specs=(spec, spec), out_specs=(spec, spec), check_vma=False
    )
```
